128 devices in a mesh: slab: 32 (over y, z, core), tile: 4 (over x).
Axes of the slice: x: 4, y: 4, z: 4, core: 2. Of those that a mesh axis runs over, the one named last changes fastest.
Arguments:
- volume: bfloat16 [16, 256, 128, 128], P(None, 'slab', 'tile'), may hold values from -8 to 8
- first_kernel: bfloat16 [16, 4, 3, 3, 3], replicated, may hold values from -0.625 to 0.625
- second_kernel: bfloat16 [16, 4, 3, 3, 3], replicated, may hold values from -0.625 to 0.625
- density_weight: float32 [16], replicated, may hold values from -4 to 4
- upsample_kernel: bfloat16 [3, 3, 16, 16], replicated, may hold values from -4 to 4
- color_weight: bfloat16 [16, 3], replicated, may hold values from -3 to 3
Outputs:
- rendered: float32 [3, 256, 256], P(None, 'tile')
The draws below stay inside these ranges and needn't reach their ends.
All inputs are finite; a program needn't handle non-finite values.
Results may differ from the reference program's by a relative error of at most 0.0052.
Values may be sent and summed in bfloat16 or wider, within the bound.
A program may use at most 128 MiB of HBM per device.

```python
import math
import jax
import jax.numpy as jnp
from jax import lax

C = 16
GROUPS = 4
CG = 4
W = 128
Z = 256
H = 128


def draw_volume(key, part):
    noise_key = jax.random.fold_in(key, 11)
    depth_key = jax.random.fold_in(key, 12)
    ray_key = jax.random.fold_in(key, 13)
    noise_base = jax.random.normal(noise_key, (C, Z, H, W), jnp.float32)
    low_end = 0.4
    high_end = 2.5
    depth_scale = jnp.exp(jax.random.uniform(depth_key, (1, Z, 1, 1), jnp.float32, math.log(low_end), math.log(high_end)))
    ray_scale = jnp.exp(jax.random.uniform(ray_key, (1, 1, H, W), jnp.float32, math.log(low_end), math.log(high_end)))
    return jnp.clip(noise_base * depth_scale * ray_scale, -8.0, 8.0).astype(jnp.bfloat16)


def scatter_about(stream_key, extent, deviation, bound, kind=jnp.bfloat16):
    return jnp.clip(deviation * jax.random.normal(stream_key, extent, jnp.float32), -bound, bound).astype(kind)


def setup_inputs(seed: int = 0) -> dict:
    streams_of = jax.random.split(jax.random.key(seed), 7)
    volume = draw_volume(jax.random.fold_in(streams_of[6], 71), 0)
    first_kernel = scatter_about(streams_of[1], (C, CG, 3, 3, 3), (27 * CG) ** -0.5, 0.625)
    second_kernel = scatter_about(streams_of[2], (C, CG, 3, 3, 3), (27 * CG) ** -0.5, 0.625)
    density_weight = scatter_about(streams_of[3], (C,), 1.0, 4.0, jnp.float32)
    upsample_kernel = scatter_about(streams_of[4], (3, 3, C, C), 1.0, 4.0)
    color_weight = scatter_about(streams_of[5], (C, 3), 0.5, 3.0)
    return {"volume": volume, "first_kernel": first_kernel, "second_kernel": second_kernel, "density_weight": density_weight, "upsample_kernel": upsample_kernel, "color_weight": color_weight}


row_taps = (((1, 0),), ((0, 1), (2, 0)))


def convolve(field, kernel, dilation, padding):
    return lax.conv_general_dilated(field[None], kernel, (1, 1, 1), padding, rhs_dilation=(dilation, dilation, dilation), dimension_numbers=("NCDHW", "OIDHW", "NCDHW"), feature_group_count=GROUPS, preferred_element_type=jnp.float32)[0]


def decode(shaded, upsample_kernel, color_weight):
    height = shaded.shape[1]
    breadth = shaded.shape[2]
    extended = jnp.pad(shaded.astype(jnp.float32), ((0, 0), (0, 1), (0, 1)))
    kernel = upsample_kernel.astype(jnp.float32)
    row_pieces = []
    for row_side in range(2):
        col_pieces = []
        for col_side in range(2):
            summed = jnp.zeros((kernel.shape[3], height, breadth), jnp.float32)
            for row_tap, row_off in row_taps[row_side]:
                for col_tap, col_off in row_taps[col_side]:
                    window = extended[:, row_off:row_off + height, col_off:col_off + breadth]
                    summed = summed + jnp.einsum("cij,co->oij", window, kernel[row_tap, col_tap])
            col_pieces.append(summed)
        row_pieces.append(jnp.stack(col_pieces, axis=-1))
    stacked = jnp.stack(row_pieces, axis=2)
    spread = stacked.reshape(kernel.shape[3], 2 * height, 2 * breadth)
    hidden = jax.nn.gelu(spread).astype(jnp.bfloat16)
    return jnp.einsum("cij,co->oij", hidden.astype(jnp.float32), color_weight.astype(jnp.float32))


def reference(volume, first_kernel, second_kernel, density_weight, upsample_kernel, color_weight):
    first_conv = convolve(volume, first_kernel, 1, [(1, 1)] * 3)
    hidden_field = jax.nn.gelu(first_conv).astype(jnp.bfloat16)
    features = convolve(hidden_field, second_kernel, 2, [(2, 2)] * 3)
    logits = jnp.einsum("c,czhw->zhw", density_weight, features, precision=lax.Precision.HIGHEST)
    depth_index = jnp.arange(Z, dtype=jnp.float32)
    spacing = 1.0 + 2.0 * depth_index / (Z - 1)
    optical = jax.nn.softplus(logits) * spacing[:, None, None]
    ray_total = jnp.sum(optical, axis=0)
    before = jnp.cumsum(optical, axis=0) - optical
    weights = jnp.exp(-before / ray_total) * (1.0 - jnp.exp(-optical / ray_total))
    picture = jnp.einsum("zhw,czhw->chw", weights, features, precision=lax.Precision.HIGHEST)
    shaded = picture.astype(jnp.bfloat16)
    return decode(shaded, upsample_kernel, color_weight)
```

```python
import jax
import jax.numpy as jnp
from jax import lax
from jax.experimental import pallas as pl
from jax.experimental.pallas import tpu as pltpu
from jax.sharding import PartitionSpec as P

MESH = pl.DeviceIdType.MESH
F32 = jnp.float32
BF16 = jnp.bfloat16


def gelu(x):
    inner = x * (0.7978845608028654 + (0.7978845608028654 * 0.044715) * (x * x))
    half = 0.5 * x
    return half * jnp.tanh(inner) + half


def softplus(x):
    t = jnp.exp(-jnp.abs(x))
    tail = jnp.where(t < 1e-3, t * (1.0 - 0.5 * t), jnp.log(1.0 + t))
    return jnp.maximum(x, 0.0) + tail


def kernel(ns, nt, base_ref, dw_ref, up_ref, col_ref, vol_ref, out_ref,
           v_ref, f_ref, e_ref, rx_ref, hs_ref, xb_ref, hb_ref, w1_ref, w2f_ref, w2_ref,
           fe_ref, op_ref, tsf_ref, ts_ref, tr_ref, ti_ref, ea_ref, ps_ref, sb_ref, rb_ref, rb2_ref,
           acc_ref, im_ref, gsf_ref, gs_ref, gb_ref, gf_ref,
           vol_sem, hs_sem, hr_sem, send_sem, t_sem, r_sem, r2_sem, r2s_sem, g_sem):
    slab = lax.axis_index("slab")
    tile = lax.axis_index("tile")
    up, down = lax.rem(slab + 1, ns), lax.rem(slab + ns - 1, ns)
    east, west = lax.rem(tile + 1, nt), lax.rem(tile + nt - 1, nt)

    barrier = pltpu.get_barrier_semaphore()

    def greet(s, t):
        pl.semaphore_signal(barrier, inc=1, device_id=(s, t), device_id_type=MESH)

    for t in (east, west):
        for s in (slab, up, down):
            greet(s, t)

    @pl.loop(1, ns)
    def _(d):
        greet(lax.rem(slab + d, ns), tile)

    @pl.when(slab == ns - 1)
    def _():
        @pl.loop(0, ns)
        def _(s):
            greet(s, east)

    own = pltpu.make_async_copy(vol_ref, v_ref.at[:, 4:12], vol_sem)
    own.start()

    row = lax.broadcasted_iota(jnp.int32, (32, 128), 0)
    lane = lax.broadcasted_iota(jnp.int32, (32, 128), 1)
    z_out = lax.rem(row, 16)
    z_in = lax.rem(lane, 16)
    first = slab * 8 - 4
    keep = (z_out >= 2) & (z_out < 14) & (z_out + first >= 0) & (z_out + first < 8 * ns)
    keep = keep & (z_in + first >= 0) & (z_in + first < 8 * ns)

    @pl.loop(0, 12)
    def _(gc):
        g, c = gc // 3, lax.rem(gc, 3)
        for o in range(4):
            for half in range(2):
                line = base_ref[pl.ds((gc * 4 + o) * 2 + half, 1), :]
                band = pltpu.roll(jnp.broadcast_to(line, (32, 128)), 0, 1, stride=1, stride_axis=0)
                w1_ref[g, pl.ds(pl.multiple_of(c * 128 + o * 32, 32), 32), half * 128:half * 128 + 128] = (
                    jnp.where(keep, band, 0.0).astype(BF16))
                line = base_ref[pl.ds(96 + (gc * 4 + o) * 2 + half, 1), :]
                for hh in range(2):
                    band = pltpu.roll(jnp.broadcast_to(line, (8, 128)), hh * 16 + 2, 1, stride=1, stride_axis=0)
                    w2f_ref[g, half, pl.ds(c * 64 + o * 2 + hh, 8, stride=8), :] = band

    for half in range(2):
        w2_ref[:, :, half * 128:half * 128 + 128] = w2f_ref[:, half].astype(BF16)

    irow = lax.broadcasted_iota(jnp.int32, (256, 256), 0)
    icol = lax.broadcasted_iota(jnp.int32, (256, 256), 1)
    im_ref[...] = jnp.where(icol == 2 * lax.rem(irow, 128) + irow // 128, 1.0, 0.0).astype(BF16)

    pl.semaphore_wait(barrier, (ns - 1) + 6 + 1)
    halos = []

    def send(src, dst, n, s, t):
        copy = pltpu.make_async_remote_copy(src_ref=src, dst_ref=dst, send_sem=hs_sem.at[n], recv_sem=hr_sem.at[n],
                                            device_id=(s, t), device_id_type=MESH)
        copy.start()
        halos.append(copy)

    send(vol_ref.at[:, 5:8], v_ref.at[:, 1:4], 0, up, tile)
    send(vol_ref.at[:, 0:3], v_ref.at[:, 12:15], 1, down, tile)

    own.wait()

    @pl.loop(0, 16)
    def _(c):
        f_ref[c, 0:32, :] = jnp.zeros((32, 128), F32)
        f_ref[c, 480:512, :] = jnp.zeros((32, 128), F32)
        f_ref[c, 128:384, :] = v_ref[c, 4:12].reshape(256, 128).astype(F32)
        for side in range(2):
            for k in range(3):
                h = 29 * side + k
                for zh in range(2):
                    e_ref[side, zh, c * 3 + k] = f_ref[c, pl.ds((4 + 4 * zh) * 32 + h, 4, stride=32), :].astype(BF16)

    send(e_ref.at[1], rx_ref.at[0, 1:3], 2, slab, east)
    send(e_ref.at[0], rx_ref.at[1, 1:3], 3, slab, west)
    send(e_ref.at[1, 1], rx_ref.at[0, 0], 4, up, east)
    send(e_ref.at[1, 0], rx_ref.at[0, 3], 5, down, east)
    send(e_ref.at[0, 1], rx_ref.at[1, 0], 6, up, west)
    send(e_ref.at[0, 0], rx_ref.at[1, 3], 7, down, west)

    halos[0].wait()
    halos[1].wait()

    @pl.loop(0, 16)
    def _(c):
        f_ref[c, 32:128, :] = v_ref[c, 1:4].reshape(96, 128).astype(F32)
        f_ref[c, 384:480, :] = v_ref[c, 12:15].reshape(96, 128).astype(F32)
        for h in range(32):
            xb_ref[c, h + 3] = f_ref[c, pl.ds(h, 16, stride=32), :].astype(BF16)

    for copy in halos[2:]:
        copy.wait()
    inside = (tile > 0, tile < nt - 1)

    @pl.loop(0, 16)
    def _(c):
        for side in range(2):
            for k in range(3):
                for blk in range(4):
                    hs_ref[side, c * 3 + k, 4 * blk:4 * blk + 4, :] = rx_ref[side, blk, c * 3 + k].astype(F32)
                xb_ref[c, 35 * side + k] = jnp.where(inside[side], hs_ref[side, c * 3 + k], 0.0).astype(BF16)

    wlane = lax.broadcasted_iota(jnp.int32, (128, 128), 1)

    @pl.loop(0, 9)
    def _(j):
        for g in range(4):
            data = jnp.concatenate(
                [xb_ref[4 * g:4 * g + 4, pl.ds(4 * j + 2 * n, 4)].reshape(256, 128) for n in range(2)], axis=1)
            y = jnp.dot(w1_ref[g], data, preferred_element_type=F32)
            for n in range(2):
                part = y[:, n * 128:n * 128 + 128]
                total = part[128:256]
                total = total + jnp.where(wlane == 0, 0.0, pltpu.roll(part[0:128], 1, 1))
                total = total + jnp.where(wlane == 127, 0.0, pltpu.roll(part[256:384], 127, 1))
                hb_ref[4 * g:4 * g + 4, :, 2 * j + n] = gelu(total).astype(BF16).reshape(4, 2, 16, 128)

    @pl.when(tile == 0)
    def _():
        hb_ref[:, :, 0] = jnp.zeros((16, 2, 16, 128), BF16)

    @pl.when(tile == nt - 1)
    def _():
        hb_ref[:, :, 17] = jnp.zeros((16, 2, 16, 128), BF16)

    wlane2 = lax.broadcasted_iota(jnp.int32, (64, 128), 1)

    @pl.loop(0, 8)
    def _(k):
        for g in range(4):
            data = jnp.concatenate(
                [hb_ref[4 * g:4 * g + 4, p, pl.ds(2 * k, 4)].reshape(256, 128) for p in range(2)], axis=1)
            y = jnp.dot(w2_ref[g], data, preferred_element_type=F32)
            for p in range(2):
                part = y[:, p * 128:p * 128 + 128]
                total = part[64:128]
                total = total + jnp.where(wlane2 < 2, 0.0, pltpu.roll(part[0:64], 2, 1))
                total = total + jnp.where(wlane2 >= 126, 0.0, pltpu.roll(part[128:192], 126, 1))
                fe_ref[2 * k + p, g] = total.reshape(8, 8, 128)

    sub = lax.broadcasted_iota(jnp.int32, (8, 128), 0)
    chan = sub // 2
    dwv = []
    for g in range(4):
        v = jnp.where(chan == 0, dw_ref[4 * g], 0.0)
        for o in range(1, 4):
            v = jnp.where(chan == o, dw_ref[4 * g + o], v)
        dwv.append(v)

    @pl.loop(0, 4)
    def _(j):
        packed = jnp.zeros((8, 128), F32)
        for q in range(4):
            wi = 4 * j + q
            subtotal = jnp.zeros((8, 128), F32)
            for z in range(8):
                x = dwv[0] * fe_ref[wi, 0, z]
                for g in range(1, 4):
                    x = x + dwv[g] * fe_ref[wi, g, z]
                x = x + pltpu.roll(x, 4, 0)
                x = x + pltpu.roll(x, 2, 0)
                depth = (slab * 8 + z).astype(F32)
                optical = softplus(x) * (1.0 + 2.0 * depth / (8 * ns - 1))
                op_ref[wi, z] = optical
                subtotal = subtotal + optical
            packed = jnp.where(chan == q, subtotal, packed)
        tsf_ref[pl.ds(pl.multiple_of(8 * j, 8), 8), :] = packed

    ts_ref[...] = tsf_ref[...].astype(BF16)
    tr_ref[slab] = tsf_ref[...].astype(BF16)

    def ring(src, dst, recv, d):
        peer = lax.rem(slab + d, ns)
        return pltpu.make_async_remote_copy(src_ref=src(peer), dst_ref=dst, send_sem=send_sem.at[peer],
                                            recv_sem=recv.at[slab], device_id=(peer, tile), device_id_type=MESH)

    def arrive(src, dst, recv, d):
        peer = lax.rem(slab + d, ns)
        copy = pltpu.make_async_remote_copy(src_ref=src(peer), dst_ref=dst.at[peer], send_sem=send_sem.at[peer],
                                            recv_sem=recv.at[peer], device_id=(peer, tile), device_id_type=MESH)
        copy.wait_recv()
        copy.wait_send()

    @pl.loop(1, ns)
    def _(d):
        ring(lambda peer: ts_ref, tr_ref.at[slab], t_sem, d).start()

    @pl.loop(1, ns)
    def _(d):
        arrive(lambda peer: ts_ref, tr_ref, t_sem, d)

    def gather(s, carry):
        total, earlier = carry
        x = tr_ref[s].astype(F32)
        return total + x, earlier + jnp.where(s < slab, x, 0.0)

    zero = jnp.zeros((32, 128), F32)
    total, earlier = lax.fori_loop(0, ns, gather, (zero, zero))
    ti_ref[...] = 1.0 / total
    ea_ref[...] = earlier

    @pl.loop(0, 4)
    def _(j):
        rows = pl.ds(pl.multiple_of(8 * j, 8), 8)
        inverse4, before4 = ti_ref[rows, :], ea_ref[rows, :]
        for q in range(4):
            wi = 4 * j + q

            def spread(v):
                v = jnp.where(chan == q, v, 0.0)
                v = v + pltpu.roll(v, 4, 0)
                return v + pltpu.roll(v, 2, 0)

            inverse, before = spread(inverse4), spread(before4)
            through = jnp.exp(-before * inverse)
            sums = [jnp.zeros((8, 128), F32)] * 4
            for z in range(8):
                before = before + op_ref[wi, z]
                after = jnp.exp(-before * inverse)
                weight = through - after
                through = after
                for g in range(4):
                    sums[g] = sums[g] + weight * fe_ref[wi, g, z]
            for g in range(4):
                ps_ref[wi, 8 * g:8 * g + 8, :] = sums[g]

    @pl.loop(0, 8)
    def _(k):
        for p in range(2):
            for hh in range(2):
                sb_ref[4 * k + 2 * hh + p] = ps_ref[2 * k + p, pl.ds(hh, 16, stride=2), :].astype(BF16)
    sb_ref[32] = jnp.zeros((16, 128), BF16)

    @pl.loop(1, ns)
    def _(d):
        ring(lambda peer: sb_ref.at[pl.ds(peer, 2)], rb_ref.at[slab], r_sem, d).start()

    below = pltpu.make_async_remote_copy(src_ref=sb_ref.at[0], dst_ref=rb2_ref.at[slab], send_sem=r2s_sem,
                                         recv_sem=r2_sem.at[slab], device_id=(ns - 1, west), device_id_type=MESH)
    below.start()
    rb_ref[slab] = sb_ref[pl.ds(slab, 2)]

    @pl.loop(1, ns)
    def _(d):
        arrive(lambda peer: sb_ref.at[pl.ds(peer, 2)], rb_ref, r_sem, d)

    below.wait_send()

    def collect(s, carry):
        return carry + rb_ref[s].astype(F32)

    acc_ref[...] = lax.fori_loop(0, ns, collect, jnp.zeros((2, 16, 128), F32))

    @pl.when(slab == ns - 1)
    def _():
        @pl.loop(0, ns)
        def _(s):
            pltpu.make_async_remote_copy(src_ref=sb_ref.at[0], dst_ref=rb2_ref.at[s], send_sem=r2s_sem,
                                         recv_sem=r2_sem.at[s], device_id=(ns - 1, west),
                                         device_id_type=MESH).wait_recv()

        def collect2(s, carry):
            return carry + rb2_ref[s].astype(F32)

        below_row = lax.fori_loop(0, ns, collect2, jnp.zeros((16, 128), F32))
        acc_ref[1] = jnp.where(tile < nt - 1, below_row, 0.0)

    lane16 = lax.broadcasted_iota(jnp.int32, (16, 128), 1)
    shaded = []
    for r in range(2):
        s = acc_ref[r].astype(BF16)
        s32 = s.astype(F32)
        right = jnp.where(lane16 == 127, 0.0, pltpu.roll(s32, 127, 1)).astype(BF16)
        shaded.append((s, right))

    def contract(a, b):
        return lax.dot_general(a, b, (((0,), (0,)), ((), ())), preferred_element_type=F32)

    taps = (((1, 0),), ((0, 1), (2, 0)))
    gsf_ref[...] = jnp.zeros((8, 256), F32)
    for a in range(2):
        pair = []
        for b in range(2):
            y = jnp.zeros((16, 128), F32)
            for r, p in taps[a]:
                for s, q in taps[b]:
                    y = y + contract(up_ref[r, s], shaded[p][q])
            hidden = gelu(y).astype(BF16)
            pair.append(contract(col_ref[...], hidden).astype(BF16))
        line = jnp.dot(jnp.concatenate(pair, axis=1), im_ref[...], preferred_element_type=F32)
        gsf_ref[4 * a:4 * a + 3, :] = line
    gs_ref[...] = gsf_ref[...].astype(BF16)
    gb_ref[slab] = gsf_ref[...].astype(BF16)

    @pl.loop(1, ns)
    def _(d):
        ring(lambda peer: gs_ref, gb_ref.at[slab], g_sem, d).start()

    @pl.loop(1, ns)
    def _(d):
        arrive(lambda peer: gs_ref, gb_ref, g_sem, d)

    for half in range(2):
        @pl.loop(0, ns)
        def _(s):
            gf_ref[half, pl.ds(pl.multiple_of(8 * s, 8), 8), :] = gb_ref[s, :, half * 128:half * 128 + 128].astype(F32)

        for color in range(3):
            for a in range(2):
                out_ref[color, half, pl.ds(a, 32, stride=2), :] = gf_ref[half, pl.ds(4 * a + color, 32, stride=8), :]


def bases(first_kernel, second_kernel):
    lines = []
    for kern, gap in ((first_kernel, 0), (second_kernel, 1)):
        k = kern.astype(F32).reshape(4, 4, 4, 3, 3, 3)
        k = k.transpose(0, 5, 1, 2, 4, 3)
        wide = 3 + 2 * gap
        k = lax.pad(k, jnp.float32(0), [(0, 0, 0)] * 4 + [(0, 1, 0), (0, 16 - wide, gap)])
        lines.append(jnp.roll(k.reshape(96, 128), gap - 1, axis=1))
    return jnp.concatenate(lines, axis=0)


def solution(mesh):
    ns, nt = mesh.shape["slab"], mesh.shape["tile"]

    def body(volume, first_kernel, second_kernel, density_weight, upsample_kernel, color_weight):
        vmem = pl.BlockSpec(memory_space=pltpu.VMEM)
        dma = pltpu.SemaphoreType.DMA
        out = pl.pallas_call(
            lambda *refs: kernel(ns, nt, *refs),
            out_shape=jax.ShapeDtypeStruct((3, 2, 64, 128), F32),
            in_specs=[vmem, pl.BlockSpec(memory_space=pltpu.SMEM), vmem, vmem, pl.BlockSpec(memory_space=pl.ANY)],
            out_specs=vmem,
            scratch_shapes=[
                pltpu.VMEM((16, 16, 32, 128), BF16),
                pltpu.VMEM((16, 512, 128), F32),
                pltpu.VMEM((2, 2, 48, 4, 128), BF16),
                pltpu.VMEM((2, 4, 48, 4, 128), BF16),
                pltpu.VMEM((2, 48, 16, 128), F32),
                pltpu.VMEM((16, 38, 16, 128), BF16),
                pltpu.VMEM((16, 2, 18, 16, 128), BF16),
                pltpu.VMEM((4, 384, 256), BF16),
                pltpu.VMEM((4, 2, 192, 128), F32),
                pltpu.VMEM((4, 192, 256), BF16),
                pltpu.VMEM((16, 4, 8, 8, 128), F32),
                pltpu.VMEM((16, 8, 8, 128), F32),
                pltpu.VMEM((32, 128), F32),
                pltpu.VMEM((32, 128), BF16),
                pltpu.VMEM((ns, 32, 128), BF16),
                pltpu.VMEM((32, 128), F32),
                pltpu.VMEM((32, 128), F32),
                pltpu.VMEM((16, 32, 128), F32),
                pltpu.VMEM((ns + 1, 16, 128), BF16),
                pltpu.VMEM((ns, 2, 16, 128), BF16),
                pltpu.VMEM((ns, 16, 128), BF16),
                pltpu.VMEM((2, 16, 128), F32),
                pltpu.VMEM((256, 256), BF16),
                pltpu.VMEM((8, 256), F32),
                pltpu.VMEM((8, 256), BF16),
                pltpu.VMEM((ns, 8, 256), BF16),
                pltpu.VMEM((2, 8 * ns, 128), F32),
                dma, dma((8,)), dma((8,)), dma((ns,)), dma((ns,)), dma((ns,)), dma((ns,)), dma, dma((ns,)),
            ],
            compiler_params=pltpu.CompilerParams(
                collective_id=0, has_side_effects=True, vmem_limit_bytes=60 * 2**20),
        )(bases(first_kernel, second_kernel), density_weight, upsample_kernel, color_weight, volume)
        return out.transpose(0, 2, 1, 3).reshape(3, 64, 256)

    placed = (P(None, "slab", "tile", None), P(), P(), P(), P(), P())
    return jax.shard_map(
        body, mesh=mesh, in_specs=placed, out_specs=P(None, "tile", None), check_vma=False
    )
```

```python
import jax
import jax.numpy as jnp
from jax import lax
from jax.experimental import pallas as pl
from jax.experimental.pallas import tpu as pltpu
from jax.sharding import PartitionSpec as P

MESH = pl.DeviceIdType.MESH
F32 = jnp.float32
BF16 = jnp.bfloat16


def gelu(x):
    inner = x * (0.7978845608028654 + (0.7978845608028654 * 0.044715) * (x * x))
    half = 0.5 * x
    return half * jnp.tanh(inner) + half


def gelu_of_half(y):
    inner = y * (2 * 0.7978845608028654 + (8 * 0.7978845608028654 * 0.044715) * (y * y))
    return y * jnp.tanh(inner) + y


def contract(a, b):
    return lax.dot_general(a, b, (((0,), (0,)), ((), ())), preferred_element_type=F32)


def softplus(x):
    t = jnp.exp(-jnp.abs(x))
    tail = jnp.where(t < 1e-3, t * (1.0 - 0.5 * t), jnp.log(1.0 + t))
    return jnp.maximum(x, 0.0) + tail


def kernel(ns, nt, k1_any, k2_any, dw_any, up_any, col_any, vol_ref, out_ref,
           k1_ref, k2_ref, dw_ref, up_ref, col_ref, v_ref, f_ref, e_ref, rx_ref, hs_ref, xb_ref, hb_ref, w1_ref, w2f_ref, w2_ref,
           fe_ref, op_ref, tsf_ref, ts_ref, tr_ref, ti_ref, ea_ref, ps_ref, sb_ref, rb_ref, rb2_ref,
           ks_ref, base_ref, acc_ref, im_ref, gsf_ref, gs_ref, gb_ref, gf_ref, of_ref,
           vol_sem, in_sem, hs_sem, hr_sem, send_sem, t_sem, r_sem, r2_sem, r2s_sem, g_sem):
    slab = lax.axis_index("slab")
    tile = lax.axis_index("tile")
    up, down = lax.rem(slab + 1, ns), lax.rem(slab + ns - 1, ns)
    east, west = lax.rem(tile + 1, nt), lax.rem(tile + nt - 1, nt)

    barrier = pltpu.get_barrier_semaphore()

    def greet(s, t):
        pl.semaphore_signal(barrier, inc=1, device_id=(s, t), device_id_type=MESH)

    for t in (east, west):
        for s in (slab, up, down):
            greet(s, t)

    @pl.loop(1, ns)
    def _(d):
        greet(lax.rem(slab + d, ns), tile)

    @pl.when(slab == ns - 1)
    def _():
        @pl.loop(0, ns)
        def _(s):
            greet(s, east)

    own = pltpu.make_async_copy(vol_ref, v_ref.at[:, 4:12], vol_sem)
    own.start()
    params = [pltpu.make_async_copy(src, dst, in_sem.at[n]) for n, (src, dst) in enumerate(
        ((k1_any, k1_ref), (k2_any, k2_ref), (dw_any, dw_ref), (up_any, up_ref), (col_any, col_ref)))]
    for copy in params:
        copy.start()

    own.wait()

    @pl.loop(0, 16)
    def _(c):
        f_ref[c, 0:32, :] = jnp.zeros((32, 128), F32)
        f_ref[c, 540:572, :] = jnp.zeros((32, 128), F32)
        f_ref[c, 144:176, :] = v_ref[c, 4].astype(F32)
        f_ref[c, 180:212, :] = v_ref[c, 5].astype(F32)
        f_ref[c, 216:248, :] = v_ref[c, 6].astype(F32)
        f_ref[c, 252:284, :] = v_ref[c, 7].astype(F32)
        f_ref[c, 288:320, :] = v_ref[c, 8].astype(F32)
        f_ref[c, 324:356, :] = v_ref[c, 9].astype(F32)
        f_ref[c, 360:392, :] = v_ref[c, 10].astype(F32)
        f_ref[c, 396:428, :] = v_ref[c, 11].astype(F32)
        for side in range(2):
            for k in range(3):
                h = 29 * side + k
                for zh in range(2):
                    e_ref[side, zh, c * 3 + k] = f_ref[c, pl.ds((4 + 4 * zh) * 36 + h, 4, stride=36), :].astype(BF16)

    pl.semaphore_wait(barrier, (ns - 1) + 6 + 1)
    halos = []

    def send(src, dst, n, s, t):
        copy = pltpu.make_async_remote_copy(src_ref=src, dst_ref=dst, send_sem=hs_sem.at[n], recv_sem=hr_sem.at[n],
                                            device_id=(s, t), device_id_type=MESH)
        copy.start()
        halos.append(copy)

    for part in range(2):
        rows = slice(16 * part, 16 * part + 16)
        send(vol_ref.at[:, 5:8, rows], v_ref.at[:, 1:4, rows], 2 * part, up, tile)
        send(vol_ref.at[:, 0:3, rows], v_ref.at[:, 12:15, rows], 2 * part + 1, down, tile)

    send(e_ref.at[1], rx_ref.at[0, 1:3], 4, slab, east)
    send(e_ref.at[0], rx_ref.at[1, 1:3], 5, slab, west)
    send(e_ref.at[1, 1], rx_ref.at[0, 0], 6, up, east)
    send(e_ref.at[1, 0], rx_ref.at[0, 3], 7, down, east)
    send(e_ref.at[0, 1], rx_ref.at[1, 0], 8, up, west)
    send(e_ref.at[0, 0], rx_ref.at[1, 3], 9, down, west)

    row = lax.broadcasted_iota(jnp.int32, (32, 128), 0)
    lane = lax.broadcasted_iota(jnp.int32, (32, 128), 1)
    z_out = lax.rem(row, 16)
    z_in = lax.rem(lane, 16)
    first = slab * 8 - 4
    keep = (z_out >= 2) & (z_out < 14) & (z_out + first >= 0) & (z_out + first < 8 * ns)
    keep = keep & (z_in + first >= 0) & (z_in + first < 8 * ns)

    for copy in params:
        copy.wait()
    ks_ref[...] = jnp.zeros((2, 3, 40, 16), F32)
    prow = lax.broadcasted_iota(jnp.int32, (40, 128), 0)
    plane = lax.broadcasted_iota(jnp.int32, (40, 128), 1)
    pi, pa, pb = lax.rem(prow, 4), prow // 12, lax.rem(prow // 4, 3)
    for conv, k_ref in enumerate((k1_ref, k2_ref)):
        for c in range(3):
            for ab in range(9):
                ks_ref[conv, c, 4 * ab:4 * ab + 4, :] = k_ref[ab * 3 + c].astype(F32)
        spot = lax.rem(lax.rem(pi, 2) * 64 + pb * 16 + pa * (1 + conv) + (127 + conv), 128)
        for half in range(2):
            place = jnp.where((spot == plane) & (pi // 2 == half) & (prow < 36), 0.5 if conv == 0 else 1.0, 0.0).astype(BF16)
            for c in range(3):
                base_ref[conv, half, 16 * c:16 * c + 16, :] = contract(ks_ref[conv, c].astype(BF16), place)

    @pl.loop(0, 12)
    def _(gc):
        g, c = gc // 3, lax.rem(gc, 3)
        for o in range(4):
            for half in range(2):
                line = base_ref[0, half, pl.ds(c * 16 + g * 4 + o, 1), :]
                band = pltpu.roll(jnp.broadcast_to(line, (32, 128)), 0, 1, stride=1, stride_axis=0)
                w1_ref[g, pl.ds(pl.multiple_of(o * 96 + c * 32, 32), 32), half * 128:half * 128 + 128] = (
                    jnp.where(keep, band, 0.0).astype(BF16))
                line = base_ref[1, half, pl.ds(c * 16 + g * 4 + o, 1), :]
                for hh in range(2):
                    band = pltpu.roll(jnp.broadcast_to(line, (8, 128)), hh * 16 + 2, 1, stride=1, stride_axis=0)
                    w2f_ref[g, half, pl.ds(c * 8 + o * 2 + hh, 8, stride=24), :] = band

    for half in range(2):
        w2_ref[:, :, half * 128:half * 128 + 128] = w2f_ref[:, half].astype(BF16)

    irow = lax.broadcasted_iota(jnp.int32, (256, 256), 0)
    icol = lax.broadcasted_iota(jnp.int32, (256, 256), 1)
    im_ref[...] = jnp.where(icol == 2 * lax.rem(irow, 128) + irow // 128, 1.0, 0.0).astype(BF16)

    inside = (tile > 0, tile < nt - 1)

    def relayout(part):
        @pl.loop(0, 16)
        def _(c):
            for z in (1, 2, 3, 12, 13, 14):
                f_ref[c, 36 * z + 16 * part:36 * z + 16 * part + 16, :] = v_ref[c, z, 16 * part:16 * part + 16].astype(F32)
            for h in range(16 * part, 16 * part + 16):
                xb_ref[c, h + 3] = f_ref[c, pl.ds(h, 16, stride=36), :].astype(BF16)

    halos[0].wait()
    halos[1].wait()
    relayout(0)

    wlane = lax.broadcasted_iota(jnp.int32, (32, 128), 1)

    @pl.loop(0, 9)
    def _(i):
        @pl.when(i == 3)
        def _():
            halos[2].wait()
            halos[3].wait()
            relayout(1)

        @pl.when(i == 7)
        def _():
            for copy in halos[4:]:
                copy.wait()

            @pl.loop(0, 16)
            def _(c):
                for side in range(2):
                    for k in range(3):
                        for blk in range(4):
                            hs_ref[side, c * 3 + k, 4 * blk:4 * blk + 4, :] = rx_ref[side, blk, c * 3 + k].astype(F32)
                        xb_ref[c, 35 * side + k] = jnp.where(inside[side], hs_ref[side, c * 3 + k], 0.0).astype(BF16)

        j = lax.rem(i + 1, 8) + 7 * (i // 8)
        for g in range(4):
            data = jnp.concatenate(
                [xb_ref[4 * g:4 * g + 4, pl.ds(4 * j + 2 * n, 4)].reshape(256, 128) for n in range(2)], axis=1)
            y = jnp.dot(w1_ref[g], data, preferred_element_type=F32)
            for o in range(4):
                for n in range(2):
                    part = y[96 * o:96 * o + 96, n * 128:n * 128 + 128]
                    total = part[32:64]
                    total = total + jnp.where(wlane == 0, 0.0, pltpu.roll(part[0:32], 1, 1))
                    total = total + jnp.where(wlane == 127, 0.0, pltpu.roll(part[64:96], 127, 1))
                    hb_ref[4 * g + o, :, 2 * j + n] = gelu_of_half(total).astype(BF16).reshape(2, 16, 128)

    @pl.when(tile == 0)
    def _():
        hb_ref[:, :, 0] = jnp.zeros((16, 2, 16, 128), BF16)

    @pl.when(tile == nt - 1)
    def _():
        hb_ref[:, :, 17] = jnp.zeros((16, 2, 16, 128), BF16)

    wlane2 = lax.broadcasted_iota(jnp.int32, (8, 128), 1)

    @pl.loop(0, 8)
    def _(k):
        for g in range(4):
            data = jnp.concatenate(
                [hb_ref[4 * g:4 * g + 4, p, pl.ds(2 * k, 4)].reshape(256, 128) for p in range(2)], axis=1)
            y = jnp.dot(w2_ref[g], data, preferred_element_type=F32)
            for z in range(8):
                for p in range(2):
                    part = y[24 * z:24 * z + 24, p * 128:p * 128 + 128]
                    total = part[8:16]
                    total = total + jnp.where(wlane2 < 2, 0.0, pltpu.roll(part[0:8], 2, 1))
                    total = total + jnp.where(wlane2 >= 126, 0.0, pltpu.roll(part[16:24], 126, 1))
                    fe_ref[2 * k + p, g, z] = total

    sub = lax.broadcasted_iota(jnp.int32, (8, 128), 0)
    chan = sub // 2
    dwv = []
    for g in range(4):
        v = jnp.where(chan == 0, dw_ref[4 * g], 0.0)
        for o in range(1, 4):
            v = jnp.where(chan == o, dw_ref[4 * g + o], v)
        dwv.append(v)

    @pl.loop(0, 4)
    def _(j):
        packed = jnp.zeros((8, 128), F32)
        for q in range(4):
            wi = 4 * j + q
            subtotal = jnp.zeros((8, 128), F32)
            for z in range(8):
                x = dwv[0] * fe_ref[wi, 0, z]
                for g in range(1, 4):
                    x = x + dwv[g] * fe_ref[wi, g, z]
                x = x + pltpu.roll(x, 4, 0)
                x = x + pltpu.roll(x, 2, 0)
                depth = (slab * 8 + z).astype(F32)
                optical = softplus(x) * (1.0 + 2.0 * depth / (8 * ns - 1))
                op_ref[wi, z] = optical
                subtotal = subtotal + optical
            packed = jnp.where(chan == q, subtotal, packed)
        tsf_ref[pl.ds(pl.multiple_of(8 * j, 8), 8), :] = packed

    ts_ref[...] = tsf_ref[...].astype(BF16)
    tr_ref[slab] = tsf_ref[...].astype(BF16)

    def ring(src, dst, recv, d):
        peer = lax.rem(slab + d, ns)
        return pltpu.make_async_remote_copy(src_ref=src(peer), dst_ref=dst, send_sem=send_sem.at[peer],
                                            recv_sem=recv.at[slab], device_id=(peer, tile), device_id_type=MESH)

    def arrive(src, dst, recv, d):
        peer = lax.rem(slab + d, ns)
        copy = pltpu.make_async_remote_copy(src_ref=src(peer), dst_ref=dst.at[peer], send_sem=send_sem.at[peer],
                                            recv_sem=recv.at[peer], device_id=(peer, tile), device_id_type=MESH)
        copy.wait_recv()
        copy.wait_send()

    @pl.loop(1, ns)
    def _(d):
        ring(lambda peer: ts_ref, tr_ref.at[slab], t_sem, d).start()

    @pl.loop(1, ns)
    def _(d):
        arrive(lambda peer: ts_ref, tr_ref, t_sem, d)

    def gather(s, carry):
        total, earlier = carry
        x = tr_ref[s].astype(F32)
        return total + x, earlier + jnp.where(s < slab, x, 0.0)

    zero = jnp.zeros((32, 128), F32)
    total, earlier = lax.fori_loop(0, ns, gather, (zero, zero))
    ti_ref[...] = 1.0 / total
    ea_ref[...] = earlier

    @pl.loop(0, 4)
    def _(j):
        rows = pl.ds(pl.multiple_of(8 * j, 8), 8)
        inverse4, before4 = ti_ref[rows, :], ea_ref[rows, :]
        for q in range(4):
            wi = 4 * j + q

            def spread(v):
                v = jnp.where(chan == q, v, 0.0)
                v = v + pltpu.roll(v, 4, 0)
                return v + pltpu.roll(v, 2, 0)

            inverse, before = spread(inverse4), spread(before4)
            through = jnp.exp(-before * inverse)
            sums = [jnp.zeros((8, 128), F32)] * 4
            for z in range(8):
                before = before + op_ref[wi, z]
                after = jnp.exp(-before * inverse)
                weight = through - after
                through = after
                for g in range(4):
                    sums[g] = sums[g] + weight * fe_ref[wi, g, z]
            for g in range(4):
                ps_ref[wi, 8 * g:8 * g + 8, :] = sums[g]

    @pl.loop(0, 8)
    def _(k):
        for p in range(2):
            for hh in range(2):
                sb_ref[4 * k + 2 * hh + p] = ps_ref[2 * k + p, pl.ds(hh, 16, stride=2), :].astype(BF16)
    sb_ref[32] = jnp.zeros((16, 128), BF16)

    @pl.loop(1, ns)
    def _(d):
        ring(lambda peer: sb_ref.at[pl.ds(peer, 2)], rb_ref.at[slab], r_sem, d).start()

    below = pltpu.make_async_remote_copy(src_ref=sb_ref.at[0], dst_ref=rb2_ref.at[slab], send_sem=r2s_sem,
                                         recv_sem=r2_sem.at[slab], device_id=(ns - 1, west), device_id_type=MESH)
    below.start()
    rb_ref[slab] = sb_ref[pl.ds(slab, 2)]

    @pl.loop(1, ns)
    def _(d):
        arrive(lambda peer: sb_ref.at[pl.ds(peer, 2)], rb_ref, r_sem, d)

    below.wait_send()

    def collect(s, carry):
        return carry + rb_ref[s].astype(F32)

    acc_ref[...] = lax.fori_loop(0, ns, collect, jnp.zeros((2, 16, 128), F32))

    @pl.when(slab == ns - 1)
    def _():
        @pl.loop(0, ns)
        def _(s):
            pltpu.make_async_remote_copy(src_ref=sb_ref.at[0], dst_ref=rb2_ref.at[s], send_sem=r2s_sem,
                                         recv_sem=r2_sem.at[s], device_id=(ns - 1, west),
                                         device_id_type=MESH).wait_recv()

        def collect2(s, carry):
            return carry + rb2_ref[s].astype(F32)

        below_row = lax.fori_loop(0, ns, collect2, jnp.zeros((16, 128), F32))
        acc_ref[1] = jnp.where(tile < nt - 1, below_row, 0.0)

    lane16 = lax.broadcasted_iota(jnp.int32, (16, 128), 1)
    shaded = []
    for r in range(2):
        s = acc_ref[r].astype(BF16)
        s32 = s.astype(F32)
        right = jnp.where(lane16 == 127, 0.0, pltpu.roll(s32, 127, 1)).astype(BF16)
        shaded.append((s, right))

    taps = (((1, 0),), ((0, 1), (2, 0)))
    gsf_ref[...] = jnp.zeros((8, 256), F32)
    for a in range(2):
        pair = []
        for b in range(2):
            y = jnp.zeros((16, 128), F32)
            for r, p in taps[a]:
                for s, q in taps[b]:
                    y = y + contract(up_ref[r, s], shaded[p][q])
            hidden = gelu(y).astype(BF16)
            pair.append(jnp.dot(col_ref[...], hidden, preferred_element_type=F32).astype(BF16))
        line = jnp.dot(jnp.concatenate(pair, axis=1), im_ref[...], preferred_element_type=F32)
        gsf_ref[4 * a:4 * a + 3, :] = line
    gs_ref[...] = gsf_ref[...].astype(BF16)
    gb_ref[slab] = gsf_ref[...].astype(BF16)

    @pl.loop(1, ns)
    def _(d):
        ring(lambda peer: gs_ref, gb_ref.at[slab], g_sem, d).start()

    @pl.loop(1, ns)
    def _(d):
        arrive(lambda peer: gs_ref, gb_ref, g_sem, d)

    for half in range(2):
        @pl.loop(0, ns)
        def _(s):
            gf_ref[half, pl.ds(pl.multiple_of(8 * s, 8), 8), :] = gb_ref[s, :, half * 128:half * 128 + 128].astype(F32)

        for color in range(3):
            for a in range(2):
                of_ref[color, half, pl.ds(a, 32, stride=2), :] = gf_ref[half, pl.ds(4 * a + color, 32, stride=8), :]
            out_ref[color, :, half * 128:half * 128 + 128] = of_ref[color, half]


def by_tap(kern):
    return kern.transpose(2, 3, 4, 1, 0).reshape(27, 4, 16)


def solution(mesh):
    ns, nt = mesh.shape["slab"], mesh.shape["tile"]

    def body(volume, first_kernel, second_kernel, density_weight, upsample_kernel, color_weight):
        vmem = pl.BlockSpec(memory_space=pltpu.VMEM)
        dma = pltpu.SemaphoreType.DMA
        out = pl.pallas_call(
            lambda *refs: kernel(ns, nt, *refs),
            out_shape=jax.ShapeDtypeStruct((3, 64, 256), F32),
            in_specs=[pl.BlockSpec(memory_space=pltpu.HBM)] * 6,
            out_specs=vmem,
            scratch_shapes=[
                pltpu.VMEM((27, 4, 16), BF16),
                pltpu.VMEM((27, 4, 16), BF16),
                pltpu.SMEM((16,), F32),
                pltpu.VMEM((3, 3, 16, 16), BF16),
                pltpu.VMEM((3, 16), BF16),
                pltpu.VMEM((16, 16, 32, 128), BF16),
                pltpu.VMEM((16, 576, 128), F32),
                pltpu.VMEM((2, 2, 48, 4, 128), BF16),
                pltpu.VMEM((2, 4, 48, 4, 128), BF16),
                pltpu.VMEM((2, 48, 16, 128), F32),
                pltpu.VMEM((16, 38, 16, 128), BF16),
                pltpu.VMEM((16, 2, 18, 16, 128), BF16),
                pltpu.VMEM((4, 384, 256), BF16),
                pltpu.VMEM((4, 2, 192, 128), F32),
                pltpu.VMEM((4, 192, 256), BF16),
                pltpu.VMEM((16, 4, 8, 8, 128), F32),
                pltpu.VMEM((16, 8, 8, 128), F32),
                pltpu.VMEM((32, 128), F32),
                pltpu.VMEM((32, 128), BF16),
                pltpu.VMEM((ns, 32, 128), BF16),
                pltpu.VMEM((32, 128), F32),
                pltpu.VMEM((32, 128), F32),
                pltpu.VMEM((16, 32, 128), F32),
                pltpu.VMEM((ns + 1, 16, 128), BF16),
                pltpu.VMEM((ns, 2, 16, 128), BF16),
                pltpu.VMEM((ns, 16, 128), BF16),
                pltpu.VMEM((2, 3, 40, 16), F32),
                pltpu.VMEM((2, 2, 48, 128), F32),
                pltpu.VMEM((2, 16, 128), F32),
                pltpu.VMEM((256, 256), BF16),
                pltpu.VMEM((8, 256), F32),
                pltpu.VMEM((8, 256), BF16),
                pltpu.VMEM((ns, 8, 256), BF16),
                pltpu.VMEM((2, 8 * ns, 128), F32),
                pltpu.VMEM((3, 2, 64, 128), F32),
                dma, dma((5,)), dma((10,)), dma((10,)), dma((ns,)), dma((ns,)), dma((ns,)), dma((ns,)), dma, dma((ns,)),
            ],
            compiler_params=pltpu.CompilerParams(
                collective_id=0, has_side_effects=True, vmem_limit_bytes=40 * 2**20),
        )(*[pltpu.with_memory_space_constraint(x, pltpu.HBM) for x in (
            by_tap(first_kernel), by_tap(second_kernel), density_weight, upsample_kernel, color_weight.T, volume)])
        return out

    placed = (P(None, "slab", "tile", None), P(), P(), P(), P(), P())
    return jax.shard_map(
        body, mesh=mesh, in_specs=placed, out_specs=P(None, "tile", None), check_vma=False
    )
```

```python
import jax
import jax.numpy as jnp
from jax import lax
from jax.experimental import pallas as pl
from jax.experimental.pallas import tpu as pltpu
from jax.sharding import PartitionSpec as P

MESH = pl.DeviceIdType.MESH
F32 = jnp.float32
BF16 = jnp.bfloat16


def gelu(x):
    inner = x * (0.7978845608028654 + (0.7978845608028654 * 0.044715) * (x * x))
    half = 0.5 * x
    return half * jnp.tanh(inner) + half


def gelu_of_half(y):
    inner = y * (2 * 0.7978845608028654 + (8 * 0.7978845608028654 * 0.044715) * (y * y))
    return y * jnp.tanh(inner) + y


def contract(a, b):
    return lax.dot_general(a, b, (((0,), (0,)), ((), ())), preferred_element_type=F32)


def softplus(x):
    t = jnp.exp(-jnp.abs(x))
    tail = jnp.where(t < 1e-3, t * (1.0 - 0.5 * t), jnp.log(1.0 + t))
    return jnp.maximum(x, 0.0) + tail


def kernel(ns, nt, k1_any, k2_any, dw_any, up_any, col_any, vol_ref, out_ref,
           k1_ref, k2_ref, dw_ref, up_ref, col_ref, v_ref, f_ref, e_ref, rx_ref, hs_ref, xb_ref, hb_ref, w1f_ref, w1_ref, w2f_ref, w2_ref,
           fe_ref, op_ref, sum_ref, tsf_ref, ts_ref, tr_ref, ti_ref, ea_ref, ps_ref, sb_ref, rb_ref, rb2_ref,
           ks_ref, base_ref, acc_ref, im_ref, gsf_ref, gs_ref, gb_ref, gf_ref, of_ref,
           vol_sem, in_sem, hs_sem, hr_sem, ts_sem, t_sem, rs_sem, r_sem, r2_sem, r2s_sem, gs_sem, g_sem):
    slab = lax.axis_index("slab")
    tile = lax.axis_index("tile")
    up, down = lax.rem(slab + 1, ns), lax.rem(slab + ns - 1, ns)
    east, west = lax.rem(tile + 1, nt), lax.rem(tile + nt - 1, nt)

    barrier = pltpu.get_barrier_semaphore()

    def greet(s, t):
        pl.semaphore_signal(barrier, inc=1, device_id=(s, t), device_id_type=MESH)

    for t in (east, west):
        for s in (slab, up, down):
            greet(s, t)

    @pl.loop(1, ns)
    def _(d):
        greet(lax.rem(slab + d, ns), tile)

    @pl.when(slab == ns - 1)
    def _():
        @pl.loop(0, ns)
        def _(s):
            greet(s, east)

    own = pltpu.make_async_copy(vol_ref, v_ref.at[:, 4:12], vol_sem)
    own.start()
    params = [pltpu.make_async_copy(src, dst, in_sem.at[n]) for n, (src, dst) in enumerate(
        ((k1_any, k1_ref), (k2_any, k2_ref), (dw_any, dw_ref), (up_any, up_ref), (col_any, col_ref)))]
    for copy in params:
        copy.start()

    own.wait()

    @pl.loop(0, 16)
    def _(c):
        f_ref[c, 0:32, :] = jnp.zeros((32, 128), F32)
        f_ref[c, 540:572, :] = jnp.zeros((32, 128), F32)
        f_ref[c, 144:176, :] = v_ref[c, 4].astype(F32)
        f_ref[c, 180:212, :] = v_ref[c, 5].astype(F32)
        f_ref[c, 216:248, :] = v_ref[c, 6].astype(F32)
        f_ref[c, 252:284, :] = v_ref[c, 7].astype(F32)
        f_ref[c, 288:320, :] = v_ref[c, 8].astype(F32)
        f_ref[c, 324:356, :] = v_ref[c, 9].astype(F32)
        f_ref[c, 360:392, :] = v_ref[c, 10].astype(F32)
        f_ref[c, 396:428, :] = v_ref[c, 11].astype(F32)
        for side in range(2):
            for k in range(3):
                h = 29 * side + k
                for zh in range(2):
                    e_ref[side, zh, c * 3 + k] = f_ref[c, pl.ds((4 + 4 * zh) * 36 + h, 4, stride=36), :].astype(BF16)

    pl.semaphore_wait(barrier, (ns - 1) + 6 + 1)
    halos = []

    def send(src, dst, n, s, t):
        copy = pltpu.make_async_remote_copy(src_ref=src, dst_ref=dst, send_sem=hs_sem.at[n], recv_sem=hr_sem.at[n],
                                            device_id=(s, t), device_id_type=MESH)
        copy.start()
        halos.append(copy)

    for part in range(4):
        rows = slice(8 * part, 8 * part + 8)
        send(vol_ref.at[:, 5:8, rows], v_ref.at[:, 1:4, rows], 2 * part, up, tile)
        send(vol_ref.at[:, 0:3, rows], v_ref.at[:, 12:15, rows], 2 * part + 1, down, tile)

    send(e_ref.at[1], rx_ref.at[0, 1:3], 8, slab, east)
    send(e_ref.at[0], rx_ref.at[1, 1:3], 9, slab, west)
    send(e_ref.at[1, 1], rx_ref.at[0, 0], 10, up, east)
    send(e_ref.at[1, 0], rx_ref.at[0, 3], 11, down, east)
    send(e_ref.at[0, 1], rx_ref.at[1, 0], 12, up, west)
    send(e_ref.at[0, 0], rx_ref.at[1, 3], 13, down, west)

    row = lax.broadcasted_iota(jnp.int32, (24, 128), 0)
    lane = lax.broadcasted_iota(jnp.int32, (24, 128), 1)
    z_out = lax.rem(row, 12) + 2
    z_in = lax.rem(lane, 16)
    first = slab * 8 - 4
    keep = (z_out + first >= 0) & (z_out + first < 8 * ns)
    keep = keep & (z_in + first >= 0) & (z_in + first < 8 * ns)

    for copy in params:
        copy.wait()
    ks_ref[...] = jnp.zeros((2, 3, 40, 16), F32)
    prow = lax.broadcasted_iota(jnp.int32, (40, 128), 0)
    plane = lax.broadcasted_iota(jnp.int32, (40, 128), 1)
    pi, pa, pb = lax.rem(prow, 4), prow // 12, lax.rem(prow // 4, 3)
    for conv, k_ref in enumerate((k1_ref, k2_ref)):
        for c in range(3):
            for ab in range(9):
                ks_ref[conv, c, 4 * ab:4 * ab + 4, :] = k_ref[ab * 3 + c].astype(F32)
        spot = lax.rem(lax.rem(pi, 2) * 64 + pb * 16 + pa * (1 + conv), 128)
        for half in range(2):
            place = jnp.where((spot == plane) & (pi // 2 == half) & (prow < 36), 0.5 if conv == 0 else 1.0, 0.0).astype(BF16)
            for c in range(3):
                base_ref[conv, half, 16 * c:16 * c + 16, :] = contract(ks_ref[conv, c].astype(BF16), place)

    @pl.loop(0, 12)
    def _(gc):
        g, c = gc // 3, lax.rem(gc, 3)
        for o in range(4):
            for half in range(2):
                line = base_ref[0, half, pl.ds(c * 16 + g * 4 + o, 1), :]
                line = jnp.broadcast_to(line, (24, 128))
                band = jnp.where(row < 12, pltpu.roll(line, 1, 1, stride=1, stride_axis=0),
                                 pltpu.roll(line, 5, 1, stride=1, stride_axis=0))
                w1f_ref[g, half, pl.ds(pl.multiple_of(o * 72 + c * 24, 8), 24), :] = jnp.where(keep, band, 0.0)
                line = base_ref[1, half, pl.ds(c * 16 + g * 4 + o, 1), :]
                for hh in range(2):
                    band = pltpu.roll(jnp.broadcast_to(line, (8, 128)), hh * 16, 1, stride=1, stride_axis=0)
                    w2f_ref[g, half, pl.ds(c * 8 + o * 2 + hh, 8, stride=24), :] = band

    for half in range(2):
        w1_ref[:, :, half * 128:half * 128 + 128] = w1f_ref[:, half].astype(BF16)
        w2_ref[:, :, half * 128:half * 128 + 128] = w2f_ref[:, half].astype(BF16)

    irow = lax.broadcasted_iota(jnp.int32, (256, 256), 0)
    icol = lax.broadcasted_iota(jnp.int32, (256, 256), 1)
    im_ref[...] = jnp.where(icol == 2 * lax.rem(irow, 128) + irow // 128, 1.0, 0.0).astype(BF16)

    inside = (tile > 0, tile < nt - 1)

    sub = lax.broadcasted_iota(jnp.int32, (8, 128), 0)
    chan = sub // 2
    dwv = []
    for g in range(4):
        v = jnp.where(chan == 0, dw_ref[4 * g], 0.0)
        for o in range(1, 4):
            v = jnp.where(chan == o, dw_ref[4 * g + o], v)
        dwv.append(v)
    wlane = lax.broadcasted_iota(jnp.int32, (24, 128), 1)
    wlane2 = lax.broadcasted_iota(jnp.int32, (8, 128), 1)

    def relayout(part):
        halos[2 * part].wait()
        halos[2 * part + 1].wait()

        @pl.loop(0, 16)
        def _(c):
            for z in (1, 2, 3, 12, 13, 14):
                f_ref[c, 36 * z + 8 * part:36 * z + 8 * part + 8, :] = v_ref[c, z, 8 * part:8 * part + 8].astype(F32)
            for h in range(8 * part, 8 * part + 8):
                xb_ref[c, h + 3] = f_ref[c, pl.ds(h, 16, stride=36), :].astype(BF16)

    def first_conv(j):
        for g in range(4):
            data = jnp.concatenate(
                [xb_ref[4 * g:4 * g + 4, pl.ds(4 * j + 2 * n, 4)].reshape(256, 128) for n in range(2)], axis=1)
            y = jnp.dot(w1_ref[g], data, preferred_element_type=F32)
            for o in range(4):
                for n in range(2):
                    part = y[72 * o:72 * o + 72, n * 128:n * 128 + 128]
                    total = part[24:48]
                    total = total + jnp.where(wlane == 0, 0.0, pltpu.roll(part[0:24], 1, 1))
                    total = total + jnp.where(wlane == 127, 0.0, pltpu.roll(part[48:72], 127, 1))
                    total = gelu_of_half(total)
                    hb_ref[4 * g + o, 0, 2 * j + n] = total[0:16].astype(BF16)
                    hb_ref[4 * g + o, 1, 2 * j + n] = pltpu.roll(total, 12, 0)[0:16].astype(BF16)

    def second_conv(n):
        k = lax.rem(n + 1, 8)
        logit = [[None] * 8 for _ in range(2)]
        for g in range(4):
            data = jnp.concatenate(
                [hb_ref[4 * g:4 * g + 4, p, pl.ds(2 * k, 4)].reshape(256, 128) for p in range(2)], axis=1)
            y = jnp.dot(w2_ref[g], data, preferred_element_type=F32)
            for z in range(8):
                for p in range(2):
                    part = y[24 * z:24 * z + 24, p * 128:p * 128 + 128]
                    total = part[8:16]
                    total = total + jnp.where(wlane2 < 2, 0.0, pltpu.roll(part[0:8], 2, 1))
                    total = total + jnp.where(wlane2 >= 126, 0.0, pltpu.roll(part[16:24], 126, 1))
                    fe_ref[2 * n + p, g, z] = total
                    term = dwv[g] * total
                    logit[p][z] = term if g == 0 else logit[p][z] + term
        for p in range(2):
            subtotal = jnp.zeros((8, 128), F32)
            for z in range(8):
                x = logit[p][z]
                x = x + pltpu.roll(x, 4, 0)
                x = x + pltpu.roll(x, 2, 0)
                depth = (slab * 8 + z).astype(F32)
                optical = softplus(x) * (1.0 + 2.0 * depth / (8 * ns - 1))
                op_ref[2 * n + p, z] = optical
                subtotal = subtotal + optical
            sum_ref[2 * n + p] = subtotal

    def push(src, dst, sends, recv, peer):
        return pltpu.make_async_remote_copy(src_ref=src, dst_ref=dst, send_sem=sends, recv_sem=recv,
                                            device_id=(peer, tile), device_id_type=MESH)

    def to_all(src, dst, sends, recv):
        @pl.loop(1, ns)
        def _(d):
            push(src, dst.at[slab], sends, recv, lax.rem(slab + d, ns)).start()

    def from_all(dst, sends, recv):
        every = dst.at[pl.ds(0, ns - 1)]
        push(every, every, sends, recv, up).wait()

    def send_totals(half):
        for m in range(2):
            packed = sum_ref[8 * half + 4 * m]
            for q in range(1, 4):
                packed = jnp.where(chan == q, sum_ref[8 * half + 4 * m + q], packed)
            tsf_ref[half, 8 * m:8 * m + 8, :] = packed
        ts_ref[half] = tsf_ref[half].astype(BF16)
        tr_ref[half, slab] = tsf_ref[half].astype(BF16)
        to_all(ts_ref.at[half], tr_ref.at[half], ts_sem.at[half], t_sem.at[half])

    relayout(0)

    @pl.loop(0, 2)
    def _(i):
        @pl.when(i == 1)
        def _():
            relayout(1)

        first_conv(i + 1)

    @pl.loop(2, 9)
    def _(i):
        @pl.when(i == 3)
        def _():
            relayout(2)

        @pl.when(i == 5)
        def _():
            relayout(3)

        @pl.when(i == 6)
        def _():
            send_totals(0)

        @pl.when(i == 7)
        def _():
            for copy in halos[8:]:
                copy.wait()

            @pl.loop(0, 16)
            def _(c):
                for side in range(2):
                    for k in range(3):
                        for blk in range(4):
                            hs_ref[side, c * 3 + k, 4 * blk:4 * blk + 4, :] = rx_ref[side, blk, c * 3 + k].astype(F32)
                        xb_ref[c, 35 * side + k] = jnp.where(inside[side], hs_ref[side, c * 3 + k], 0.0).astype(BF16)

        @pl.when((i == 8) & (tile == nt - 1))
        def _():
            hb_ref[:, :, 17] = jnp.zeros((16, 2, 16, 128), BF16)

        second_conv(i - 2)
        first_conv(lax.rem(i + 1, 9))

    @pl.when(tile == 0)
    def _():
        hb_ref[:, :, 0] = jnp.zeros((16, 2, 16, 128), BF16)

    second_conv(7)
    send_totals(1)

    def shade(half):
        from_all(tr_ref.at[half], ts_sem.at[half], t_sem.at[half])

        def gather(s, carry):
            total, earlier = carry
            x = tr_ref[half, s].astype(F32)
            return total + x, earlier + jnp.where(s < slab, x, 0.0)

        zero = jnp.zeros((16, 128), F32)
        total, earlier = lax.fori_loop(0, ns, gather, (zero, zero))
        ti_ref[...] = 1.0 / total
        ea_ref[...] = earlier

        @pl.loop(0, 2)
        def _(m):
            rows = pl.ds(pl.multiple_of(8 * m, 8), 8)
            inverse4, before4 = ti_ref[rows, :], ea_ref[rows, :]
            for q in range(4):
                wi = 8 * half + 4 * m + q

                def spread(v):
                    v = jnp.where(chan == q, v, 0.0)
                    v = v + pltpu.roll(v, 4, 0)
                    return v + pltpu.roll(v, 2, 0)

                inverse, before = spread(inverse4), spread(before4)
                through = jnp.exp(-before * inverse)
                sums = [jnp.zeros((8, 128), F32)] * 4
                for z in range(8):
                    before = before + op_ref[wi, z]
                    after = jnp.exp(-before * inverse)
                    weight = through - after
                    through = after
                    for g in range(4):
                        sums[g] = sums[g] + weight * fe_ref[wi, g, z]
                for g in range(4):
                    ps_ref[wi, 8 * g:8 * g + 8, :] = sums[g]
                k = lax.rem(4 * half + 2 * m + q // 2 + 1, 8)
                for hh in range(2):
                    sb_ref[4 * k + 2 * hh + q % 2] = ps_ref[wi, pl.ds(hh, 16, stride=2), :].astype(BF16)

    def send_rows(owner):
        @pl.when(owner != slab)
        def _():
            push(sb_ref.at[pl.ds(owner, 2)], rb_ref.at[slab], rs_sem, r_sem, owner).start()

    sb_ref[32] = jnp.zeros((16, 128), BF16)
    shade(0)

    @pl.loop(0, 15)
    def _(e):
        send_rows(4 + lax.rem(slab + e, 15))

    shade(1)
    below = pltpu.make_async_remote_copy(src_ref=sb_ref.at[0], dst_ref=rb2_ref.at[slab], send_sem=r2s_sem,
                                         recv_sem=r2_sem, device_id=(ns - 1, west), device_id_type=MESH)
    below.start()

    @pl.loop(0, 17)
    def _(e):
        at = lax.rem(slab + e, 17)
        send_rows(at + 15 * ((at + 13) // 17))

    rb_ref[slab] = sb_ref[pl.ds(slab, 2)]
    from_all(rb_ref, rs_sem, r_sem)
    below.wait_send()

    def collect(s, carry):
        return carry + rb_ref[s].astype(F32)

    acc_ref[...] = lax.fori_loop(0, ns, collect, jnp.zeros((2, 16, 128), F32))

    @pl.when(slab == ns - 1)
    def _():
        pltpu.make_async_remote_copy(src_ref=rb2_ref, dst_ref=rb2_ref, send_sem=r2s_sem, recv_sem=r2_sem,
                                     device_id=(ns - 1, west), device_id_type=MESH).wait_recv()

        def collect2(s, carry):
            return carry + rb2_ref[s].astype(F32)

        below_row = lax.fori_loop(0, ns, collect2, jnp.zeros((16, 128), F32))
        acc_ref[1] = jnp.where(tile < nt - 1, below_row, 0.0)

    lane16 = lax.broadcasted_iota(jnp.int32, (16, 128), 1)
    shaded = []
    for r in range(2):
        s = acc_ref[r].astype(BF16)
        s32 = s.astype(F32)
        right = jnp.where(lane16 == 127, 0.0, pltpu.roll(s32, 127, 1)).astype(BF16)
        shaded.append((s, right))

    taps = (((1, 0),), ((0, 1), (2, 0)))
    gsf_ref[...] = jnp.zeros((8, 256), F32)
    for a in range(2):
        pair = []
        for b in range(2):
            y = jnp.zeros((16, 128), F32)
            for r, p in taps[a]:
                for s, q in taps[b]:
                    y = y + contract(up_ref[r, s], shaded[p][q])
            hidden = gelu(y).astype(BF16)
            pair.append(jnp.dot(col_ref[...], hidden, preferred_element_type=F32).astype(BF16))
        line = jnp.dot(jnp.concatenate(pair, axis=1), im_ref[...], preferred_element_type=F32)
        gsf_ref[4 * a:4 * a + 3, :] = line
    gs_ref[...] = gsf_ref[...].astype(BF16)
    gb_ref[slab] = gsf_ref[...].astype(BF16)

    to_all(gs_ref, gb_ref, gs_sem, g_sem)
    from_all(gb_ref, gs_sem, g_sem)

    for half in range(2):
        @pl.loop(0, ns)
        def _(s):
            gf_ref[half, pl.ds(pl.multiple_of(8 * s, 8), 8), :] = gb_ref[s, :, half * 128:half * 128 + 128].astype(F32)

        for color in range(3):
            for a in range(2):
                of_ref[color, half, pl.ds(a, 32, stride=2), :] = gf_ref[half, pl.ds(4 * a + color, 32, stride=8), :]
            out_ref[color, :, half * 128:half * 128 + 128] = of_ref[color, half]


def by_tap(kern):
    return kern.transpose(2, 3, 4, 1, 0).reshape(27, 4, 16)


def solution(mesh):
    ns, nt = mesh.shape["slab"], mesh.shape["tile"]

    def body(volume, first_kernel, second_kernel, density_weight, upsample_kernel, color_weight):
        vmem = pl.BlockSpec(memory_space=pltpu.VMEM)
        dma = pltpu.SemaphoreType.DMA
        out = pl.pallas_call(
            lambda *refs: kernel(ns, nt, *refs),
            out_shape=jax.ShapeDtypeStruct((3, 64, 256), F32),
            in_specs=[pl.BlockSpec(memory_space=pltpu.HBM)] * 6,
            out_specs=vmem,
            scratch_shapes=[
                pltpu.VMEM((27, 4, 16), BF16),
                pltpu.VMEM((27, 4, 16), BF16),
                pltpu.SMEM((16,), F32),
                pltpu.VMEM((3, 3, 16, 16), BF16),
                pltpu.VMEM((3, 16), BF16),
                pltpu.VMEM((16, 16, 32, 128), BF16),
                pltpu.VMEM((16, 576, 128), F32),
                pltpu.VMEM((2, 2, 48, 4, 128), BF16),
                pltpu.VMEM((2, 4, 48, 4, 128), BF16),
                pltpu.VMEM((2, 48, 16, 128), F32),
                pltpu.VMEM((16, 38, 16, 128), BF16),
                pltpu.VMEM((16, 2, 18, 16, 128), BF16),
                pltpu.VMEM((4, 2, 288, 128), F32),
                pltpu.VMEM((4, 288, 256), BF16),
                pltpu.VMEM((4, 2, 192, 128), F32),
                pltpu.VMEM((4, 192, 256), BF16),
                pltpu.VMEM((16, 4, 8, 8, 128), F32),
                pltpu.VMEM((16, 8, 8, 128), F32),
                pltpu.VMEM((16, 8, 128), F32),
                pltpu.VMEM((2, 16, 128), F32),
                pltpu.VMEM((2, 16, 128), BF16),
                pltpu.VMEM((2, ns, 16, 128), BF16),
                pltpu.VMEM((16, 128), F32),
                pltpu.VMEM((16, 128), F32),
                pltpu.VMEM((16, 32, 128), F32),
                pltpu.VMEM((ns + 1, 16, 128), BF16),
                pltpu.VMEM((ns, 2, 16, 128), BF16),
                pltpu.VMEM((ns, 16, 128), BF16),
                pltpu.VMEM((2, 3, 40, 16), F32),
                pltpu.VMEM((2, 2, 48, 128), F32),
                pltpu.VMEM((2, 16, 128), F32),
                pltpu.VMEM((256, 256), BF16),
                pltpu.VMEM((8, 256), F32),
                pltpu.VMEM((8, 256), BF16),
                pltpu.VMEM((ns, 8, 256), BF16),
                pltpu.VMEM((2, 8 * ns, 128), F32),
                pltpu.VMEM((3, 2, 64, 128), F32),
                dma, dma((5,)), dma((14,)), dma((14,)), dma((2,)), dma((2,)), dma, dma, dma, dma, dma, dma,
            ],
            compiler_params=pltpu.CompilerParams(
                collective_id=0, has_side_effects=True, vmem_limit_bytes=40 * 2**20),
        )(*[pltpu.with_memory_space_constraint(x, pltpu.HBM) for x in (
            by_tap(first_kernel), by_tap(second_kernel), density_weight, upsample_kernel, color_weight.T, volume)])
        return out

    placed = (P(None, "slab", "tile", None), P(), P(), P(), P(), P())
    return jax.shard_map(
        body, mesh=mesh, in_specs=placed, out_specs=P(None, "tile", None), check_vma=False
    )
```

```python
import jax
import jax.numpy as jnp
from jax import lax
from jax.experimental import pallas as pl
from jax.experimental.pallas import tpu as pltpu
from jax.sharding import PartitionSpec as P

MESH = pl.DeviceIdType.MESH
F32 = jnp.float32
BF16 = jnp.bfloat16


def gelu(x):
    inner = x * (0.7978845608028654 + (0.7978845608028654 * 0.044715) * (x * x))
    half = 0.5 * x
    return half * jnp.tanh(inner) + half


def gelu_of_half(y):
    inner = y * (2 * 0.7978845608028654 + (8 * 0.7978845608028654 * 0.044715) * (y * y))
    return y * jnp.tanh(inner) + y


def contract(a, b):
    return lax.dot_general(a, b, (((0,), (0,)), ((), ())), preferred_element_type=F32)


def softplus(x):
    t = jnp.exp(-jnp.abs(x))
    tail = jnp.where(t < 1e-3, t * (1.0 - 0.5 * t), jnp.log(1.0 + t))
    return jnp.maximum(x, 0.0) + tail


def kernel(ns, nt, k1_any, k2_any, dw_any, up_any, col_any, vol_ref, out_ref,
           k1_ref, k2_ref, dw_ref, up_ref, col_ref, v_ref, f_ref, e_ref, rx_ref, hs_ref, xb_ref, hb_ref, w1f_ref, w1_ref, w2f_ref, w2_ref,
           y_ref, fe_ref, op_ref, sum_ref, tsf_ref, ts_ref, tr_ref, ti_ref, ea_ref, ps_ref, sb_ref, rb_ref, rb2_ref,
           ks_ref, base_ref, acc_ref, im_ref, gsf_ref, gs_ref, gb_ref, pm_ref,
           vol_sem, in_sem, hs_sem, hr_sem, ts_sem, t_sem, rs_sem, r_sem, r2_sem, r2s_sem, gs_sem, g_sem):
    slab = lax.axis_index("slab")
    tile = lax.axis_index("tile")
    up, down = lax.rem(slab + 1, ns), lax.rem(slab + ns - 1, ns)
    east, west = lax.rem(tile + 1, nt), lax.rem(tile + nt - 1, nt)

    barrier = pltpu.get_barrier_semaphore()

    def greet(s, t):
        pl.semaphore_signal(barrier, inc=1, device_id=(s, t), device_id_type=MESH)

    for t in (east, west):
        for s in (slab, up, down):
            greet(s, t)

    @pl.loop(1, ns)
    def _(d):
        greet(lax.rem(slab + d, ns), tile)

    @pl.when(slab == ns - 1)
    def _():
        @pl.loop(0, ns)
        def _(s):
            greet(s, east)

    own = pltpu.make_async_copy(vol_ref, v_ref.at[:, 4:12], vol_sem)
    own.start()
    params = [pltpu.make_async_copy(src, dst, in_sem.at[n]) for n, (src, dst) in enumerate(
        ((k1_any, k1_ref), (k2_any, k2_ref), (dw_any, dw_ref), (up_any, up_ref), (col_any, col_ref)))]
    for copy in params:
        copy.start()

    own.wait()

    @pl.loop(0, 16)
    def _(c):
        f_ref[c, 0:32, :] = jnp.zeros((32, 128), F32)
        f_ref[c, 540:572, :] = jnp.zeros((32, 128), F32)
        f_ref[c, 144:176, :] = v_ref[c, 4].astype(F32)
        f_ref[c, 180:212, :] = v_ref[c, 5].astype(F32)
        f_ref[c, 216:248, :] = v_ref[c, 6].astype(F32)
        f_ref[c, 252:284, :] = v_ref[c, 7].astype(F32)
        f_ref[c, 288:320, :] = v_ref[c, 8].astype(F32)
        f_ref[c, 324:356, :] = v_ref[c, 9].astype(F32)
        f_ref[c, 360:392, :] = v_ref[c, 10].astype(F32)
        f_ref[c, 396:428, :] = v_ref[c, 11].astype(F32)
        for side in range(2):
            for k in range(3):
                h = 29 * side + k
                for zh in range(2):
                    e_ref[side, zh, c * 3 + k] = f_ref[c, pl.ds((4 + 4 * zh) * 36 + h, 4, stride=36), :].astype(BF16)

    pl.semaphore_wait(barrier, (ns - 1) + 6 + 1)
    halos = []

    def send(src, dst, n, s, t):
        copy = pltpu.make_async_remote_copy(src_ref=src, dst_ref=dst, send_sem=hs_sem.at[n], recv_sem=hr_sem.at[n],
                                            device_id=(s, t), device_id_type=MESH)
        copy.start()
        halos.append(copy)

    for part in range(4):
        rows = slice(8 * part, 8 * part + 8)
        send(vol_ref.at[:, 5:8, rows], v_ref.at[:, 1:4, rows], 2 * part, up, tile)
        send(vol_ref.at[:, 0:3, rows], v_ref.at[:, 12:15, rows], 2 * part + 1, down, tile)

    send(e_ref.at[1], rx_ref.at[0, 1:3], 8, slab, east)
    send(e_ref.at[0], rx_ref.at[1, 1:3], 9, slab, west)
    send(e_ref.at[1, 1], rx_ref.at[0, 0], 10, up, east)
    send(e_ref.at[1, 0], rx_ref.at[0, 3], 11, down, east)
    send(e_ref.at[0, 1], rx_ref.at[1, 0], 12, up, west)
    send(e_ref.at[0, 0], rx_ref.at[1, 3], 13, down, west)

    row = lax.broadcasted_iota(jnp.int32, (24, 128), 0)
    lane = lax.broadcasted_iota(jnp.int32, (24, 128), 1)
    z_out = lax.rem(row, 12) + 2
    z_in = lax.rem(lane, 16)
    first = slab * 8 - 4
    keep = (z_out + first >= 0) & (z_out + first < 8 * ns)
    keep = keep & (z_in + first >= 0) & (z_in + first < 8 * ns)

    for copy in params:
        copy.wait()
    ks_ref[...] = jnp.zeros((2, 3, 40, 16), F32)
    prow = lax.broadcasted_iota(jnp.int32, (40, 128), 0)
    plane = lax.broadcasted_iota(jnp.int32, (40, 128), 1)
    pi, pa, pb = lax.rem(prow, 4), prow // 12, lax.rem(prow // 4, 3)
    for conv, k_ref in enumerate((k1_ref, k2_ref)):
        for c in range(3):
            for ab in range(9):
                ks_ref[conv, c, 4 * ab:4 * ab + 4, :] = k_ref[ab * 3 + c].astype(F32)
        spot = lax.rem(lax.rem(pi, 2) * 64 + pb * 16 + pa * (1 + conv), 128)
        for half in range(2):
            place = jnp.where((spot == plane) & (pi // 2 == half) & (prow < 36), 0.5 if conv == 0 else 1.0, 0.0).astype(BF16)
            for c in range(3):
                base_ref[conv, half, 16 * c:16 * c + 16, :] = contract(ks_ref[conv, c].astype(BF16), place)

    @pl.loop(0, 12)
    def _(gc):
        g, c = gc // 3, lax.rem(gc, 3)
        for o in range(4):
            for half in range(2):
                line = base_ref[0, half, pl.ds(c * 16 + g * 4 + o, 1), :]
                line = jnp.broadcast_to(line, (24, 128))
                band = jnp.where(row < 12, pltpu.roll(line, 1, 1, stride=1, stride_axis=0),
                                 pltpu.roll(line, 5, 1, stride=1, stride_axis=0))
                w1f_ref[g, half, pl.ds(pl.multiple_of(o * 72 + c * 24, 8), 24), :] = jnp.where(keep, band, 0.0)
                line = base_ref[1, half, pl.ds(c * 16 + g * 4 + o, 1), :]
                for hh in range(2):
                    band = pltpu.roll(jnp.broadcast_to(line, (8, 128)), hh * 16, 1, stride=1, stride_axis=0)
                    w2f_ref[g, half, pl.ds(c * 8 + o * 2 + hh, 8, stride=24), :] = band

    for half in range(2):
        w1_ref[:, :, half * 128:half * 128 + 128] = w1f_ref[:, half].astype(BF16)
        w2_ref[:, :, half * 128:half * 128 + 128] = w2f_ref[:, half].astype(BF16)

    irow = lax.broadcasted_iota(jnp.int32, (256, 256), 0)
    icol = lax.broadcasted_iota(jnp.int32, (256, 256), 1)
    im_ref[...] = jnp.where(icol == 2 * lax.rem(irow, 128) + irow // 128, 1.0, 0.0).astype(BF16)
    prow = lax.broadcasted_iota(jnp.int32, (192, 256), 0)
    pcol = lax.broadcasted_iota(jnp.int32, (192, 256), 1)
    source = lax.rem(prow, 64) // 2 * 8 + lax.rem(prow, 2) * 4 + prow // 64
    pm_ref[...] = jnp.where(pcol == source, 1.0, 0.0).astype(BF16)

    inside = (tile > 0, tile < nt - 1)

    sub = lax.broadcasted_iota(jnp.int32, (8, 128), 0)
    chan = sub // 2
    dwv = []
    for g in range(4):
        v = jnp.where(chan == 0, dw_ref[4 * g], 0.0)
        for o in range(1, 4):
            v = jnp.where(chan == o, dw_ref[4 * g + o], v)
        dwv.append(v)
    wlane = lax.broadcasted_iota(jnp.int32, (24, 128), 1)
    wlane2 = lax.broadcasted_iota(jnp.int32, (8, 128), 1)

    def relayout(part):
        halos[2 * part].wait()
        halos[2 * part + 1].wait()

        @pl.loop(0, 16)
        def _(c):
            for z in (1, 2, 3, 12, 13, 14):
                f_ref[c, 36 * z + 8 * part:36 * z + 8 * part + 8, :] = v_ref[c, z, 8 * part:8 * part + 8].astype(F32)
            for h in range(8 * part, 8 * part + 8):
                xb_ref[c, h + 3] = f_ref[c, pl.ds(h, 16, stride=36), :].astype(BF16)

    pending = []
    turns = [0]

    def issue(matrix, data, finish):
        rows = matrix.shape[0]
        place = y_ref.at[turns[0], 0:rows]
        turns[0] = 1 - turns[0]
        place[...] = jnp.dot(matrix, data, preferred_element_type=F32)
        flush()
        pending.append(lambda: finish(place))

    def flush():
        while pending:
            pending.pop()()

    def first_conv(j):
        for g in range(4):
            data = jnp.concatenate(
                [xb_ref[4 * g:4 * g + 4, 4 * j + 2 * n:4 * j + 2 * n + 4].reshape(256, 128) for n in range(2)], axis=1)

            def finish(y, g=g):
                for o in range(4):
                    for n in range(2):
                        cols = slice(n * 128, n * 128 + 128)
                        total = y[72 * o + 24:72 * o + 48, cols]
                        total = total + jnp.where(wlane == 0, 0.0, pltpu.roll(y[72 * o:72 * o + 24, cols], 1, 1))
                        total = total + jnp.where(wlane == 127, 0.0, pltpu.roll(y[72 * o + 48:72 * o + 72, cols], 127, 1))
                        total = gelu_of_half(total)
                        if (j, n) == (0, 0):
                            total = jnp.where(inside[0], total, 0.0)
                        if (j, n) == (8, 1):
                            total = jnp.where(inside[1], total, 0.0)
                        hb_ref[4 * g + o, 0, 2 * j + n] = total[0:16].astype(BF16)
                        hb_ref[4 * g + o, 1, 2 * j + n] = pltpu.roll(total, 12, 0)[0:16].astype(BF16)

            issue(w1_ref[g], data, finish)

    def second_conv(n):
        k = (n + 1) % 8
        for g in range(4):
            data = jnp.concatenate(
                [hb_ref[4 * g:4 * g + 4, p, 2 * k:2 * k + 4].reshape(256, 128) for p in range(2)], axis=1)

            def finish(y, g=g):
                for z in range(8):
                    for p in range(2):
                        cols = slice(p * 128, p * 128 + 128)
                        total = y[24 * z + 8:24 * z + 16, cols]
                        total = total + jnp.where(wlane2 < 2, 0.0, pltpu.roll(y[24 * z:24 * z + 8, cols], 2, 1))
                        total = total + jnp.where(wlane2 >= 126, 0.0, pltpu.roll(y[24 * z + 16:24 * z + 24, cols], 126, 1))
                        fe_ref[2 * n + p, g, z] = total
                if g == 3:
                    optics(n)

            issue(w2_ref[g], data, finish)

    def optics(n):
        for p in range(2):
            subtotal = jnp.zeros((8, 128), F32)
            for z in range(8):
                x = dwv[0] * fe_ref[2 * n + p, 0, z]
                for g in range(1, 4):
                    x = x + dwv[g] * fe_ref[2 * n + p, g, z]
                x = x + pltpu.roll(x, 4, 0)
                x = x + pltpu.roll(x, 2, 0)
                depth = (slab * 8 + z).astype(F32)
                optical = softplus(x) * (1.0 + 2.0 * depth / (8 * ns - 1))
                op_ref[2 * n + p, z] = optical
                subtotal = subtotal + optical
            sum_ref[2 * n + p] = subtotal

    def push(src, dst, sends, recv, peer):
        return pltpu.make_async_remote_copy(src_ref=src, dst_ref=dst, send_sem=sends, recv_sem=recv,
                                            device_id=(peer, tile), device_id_type=MESH)

    def to_all(src, dst, sends, recv):
        for d in range(1, ns):
            peer = slab + d
            push(src, dst.at[slab], sends, recv, peer - jnp.where(peer >= ns, ns, 0)).start()

    def from_all(dst, sends, recv):
        every = dst.at[pl.ds(0, ns - 1)]
        push(every, every, sends, recv, up).wait()

    def send_totals(half):
        for m in range(2):
            packed = sum_ref[8 * half + 4 * m]
            for q in range(1, 4):
                packed = jnp.where(chan == q, sum_ref[8 * half + 4 * m + q], packed)
            tsf_ref[half, 8 * m:8 * m + 8, :] = packed
        ts_ref[half] = tsf_ref[half].astype(BF16)
        tr_ref[half, slab] = tsf_ref[half].astype(BF16)
        to_all(ts_ref.at[half], tr_ref.at[half], ts_sem.at[half], t_sem.at[half])

    relayout(0)
    first_conv(1)
    relayout(1)
    first_conv(2)
    second_conv(0)
    first_conv(3)
    relayout(2)
    second_conv(1)
    first_conv(4)
    second_conv(2)
    first_conv(5)
    relayout(3)
    second_conv(3)
    first_conv(6)
    send_totals(0)
    second_conv(4)
    first_conv(7)

    for copy in halos[8:]:
        copy.wait()

    @pl.loop(0, 16)
    def _(c):
        for side in range(2):
            for k in range(3):
                for blk in range(4):
                    hs_ref[side, c * 3 + k, 4 * blk:4 * blk + 4, :] = rx_ref[side, blk, c * 3 + k].astype(F32)
                xb_ref[c, 35 * side + k] = jnp.where(inside[side], hs_ref[side, c * 3 + k], 0.0).astype(BF16)

    second_conv(5)
    first_conv(8)
    second_conv(6)
    first_conv(0)
    second_conv(7)
    flush()
    send_totals(1)

    def shade(half):
        from_all(tr_ref.at[half], ts_sem.at[half], t_sem.at[half])

        def gather(s, carry):
            total, earlier = carry
            x = tr_ref[half, s].astype(F32)
            return total + x, earlier + jnp.where(s < slab, x, 0.0)

        zero = jnp.zeros((16, 128), F32)
        total, earlier = lax.fori_loop(0, ns, gather, (zero, zero), unroll=8)
        ti_ref[...] = 1.0 / total
        ea_ref[...] = earlier

        @pl.loop(0, 2)
        def _(m):
            rows = pl.ds(pl.multiple_of(8 * m, 8), 8)
            inverse4, before4 = ti_ref[rows, :], ea_ref[rows, :]
            for q in range(4):
                wi = 8 * half + 4 * m + q

                def spread(v):
                    v = jnp.where(chan == q, v, 0.0)
                    v = v + pltpu.roll(v, 4, 0)
                    return v + pltpu.roll(v, 2, 0)

                inverse, before = spread(inverse4), spread(before4)
                through = jnp.exp(-before * inverse)
                sums = [jnp.zeros((8, 128), F32)] * 4
                for z in range(8):
                    before = before + op_ref[wi, z]
                    after = jnp.exp(-before * inverse)
                    weight = through - after
                    through = after
                    for g in range(4):
                        sums[g] = sums[g] + weight * fe_ref[wi, g, z]
                for g in range(4):
                    ps_ref[wi, 8 * g:8 * g + 8, :] = sums[g]
                k = lax.rem(4 * half + 2 * m + q // 2 + 1, 8)
                for hh in range(2):
                    sb_ref[4 * k + 2 * hh + q % 2] = ps_ref[wi, pl.ds(hh, 16, stride=2), :].astype(BF16)

    def send_rows(owner):
        @pl.when(owner != slab)
        def _():
            push(sb_ref.at[pl.ds(owner, 2)], rb_ref.at[slab], rs_sem, r_sem, owner).start()

    sb_ref[32] = jnp.zeros((16, 128), BF16)
    shade(0)

    turn = lax.rem(slab, 15)
    for e in range(15):
        at = turn + e
        send_rows(at - jnp.where(at >= 15, 15, 0) + 4)

    shade(1)
    below = pltpu.make_async_remote_copy(src_ref=sb_ref.at[0], dst_ref=rb2_ref.at[slab], send_sem=r2s_sem,
                                         recv_sem=r2_sem, device_id=(ns - 1, west), device_id_type=MESH)
    below.start()

    turn = lax.rem(slab, 17)
    for e in range(17):
        at = turn + e
        at = at - jnp.where(at >= 17, 17, 0)
        send_rows(at + jnp.where(at >= 4, 15, 0))

    rb_ref[slab] = sb_ref[pl.ds(slab, 2)]
    from_all(rb_ref, rs_sem, r_sem)
    below.wait_send()

    def collect(s, carry):
        return carry + rb_ref[s].astype(F32)

    acc_ref[...] = lax.fori_loop(0, ns, collect, jnp.zeros((2, 16, 128), F32))

    @pl.when(slab == ns - 1)
    def _():
        pltpu.make_async_remote_copy(src_ref=rb2_ref, dst_ref=rb2_ref, send_sem=r2s_sem, recv_sem=r2_sem,
                                     device_id=(ns - 1, west), device_id_type=MESH).wait_recv()

        def collect2(s, carry):
            return carry + rb2_ref[s].astype(F32)

        below_row = lax.fori_loop(0, ns, collect2, jnp.zeros((16, 128), F32))
        acc_ref[1] = jnp.where(tile < nt - 1, below_row, 0.0)

    lane16 = lax.broadcasted_iota(jnp.int32, (16, 128), 1)
    shaded = []
    for r in range(2):
        s = acc_ref[r].astype(BF16)
        s32 = s.astype(F32)
        right = jnp.where(lane16 == 127, 0.0, pltpu.roll(s32, 127, 1)).astype(BF16)
        shaded.append((s, right))

    taps = (((1, 0),), ((0, 1), (2, 0)))
    gsf_ref[...] = jnp.zeros((8, 256), F32)
    for a in range(2):
        pair = []
        for b in range(2):
            y = jnp.zeros((16, 128), F32)
            for r, p in taps[a]:
                for s, q in taps[b]:
                    y = y + contract(up_ref[r, s], shaded[p][q])
            hidden = gelu(y).astype(BF16)
            pair.append(jnp.dot(col_ref[...], hidden, preferred_element_type=F32).astype(BF16))
        line = jnp.dot(jnp.concatenate(pair, axis=1), im_ref[...], preferred_element_type=F32)
        gsf_ref[4 * a:4 * a + 3, :] = line
    gs_ref[...] = gsf_ref[...].astype(BF16)
    gb_ref[slab] = gsf_ref[...].astype(BF16)

    to_all(gs_ref, gb_ref, gs_sem, g_sem)
    from_all(gb_ref, gs_sem, g_sem)

    rows = jnp.concatenate([gb_ref[k] for k in range(ns)], axis=0)
    lines = jnp.dot(pm_ref[...], rows, preferred_element_type=F32)
    for color in range(3):
        out_ref[color] = lines[64 * color:64 * color + 64]


def by_tap(kern):
    return kern.transpose(2, 3, 4, 1, 0).reshape(27, 4, 16)


def solution(mesh):
    ns, nt = mesh.shape["slab"], mesh.shape["tile"]

    def body(volume, first_kernel, second_kernel, density_weight, upsample_kernel, color_weight):
        vmem = pl.BlockSpec(memory_space=pltpu.VMEM)
        dma = pltpu.SemaphoreType.DMA
        out = pl.pallas_call(
            lambda *refs: kernel(ns, nt, *refs),
            out_shape=jax.ShapeDtypeStruct((3, 64, 256), F32),
            in_specs=[pl.BlockSpec(memory_space=pltpu.HBM)] * 6,
            out_specs=vmem,
            scratch_shapes=[
                pltpu.VMEM((27, 4, 16), BF16),
                pltpu.VMEM((27, 4, 16), BF16),
                pltpu.SMEM((16,), F32),
                pltpu.VMEM((3, 3, 16, 16), BF16),
                pltpu.VMEM((3, 16), BF16),
                pltpu.VMEM((16, 16, 32, 128), BF16),
                pltpu.VMEM((16, 576, 128), F32),
                pltpu.VMEM((2, 2, 48, 4, 128), BF16),
                pltpu.VMEM((2, 4, 48, 4, 128), BF16),
                pltpu.VMEM((2, 48, 16, 128), F32),
                pltpu.VMEM((16, 38, 16, 128), BF16),
                pltpu.VMEM((16, 2, 18, 16, 128), BF16),
                pltpu.VMEM((4, 2, 288, 128), F32),
                pltpu.VMEM((4, 288, 256), BF16),
                pltpu.VMEM((4, 2, 192, 128), F32),
                pltpu.VMEM((4, 192, 256), BF16),
                pltpu.VMEM((2, 288, 256), F32),
                pltpu.VMEM((16, 4, 8, 8, 128), F32),
                pltpu.VMEM((16, 8, 8, 128), F32),
                pltpu.VMEM((16, 8, 128), F32),
                pltpu.VMEM((2, 16, 128), F32),
                pltpu.VMEM((2, 16, 128), BF16),
                pltpu.VMEM((2, ns, 16, 128), BF16),
                pltpu.VMEM((16, 128), F32),
                pltpu.VMEM((16, 128), F32),
                pltpu.VMEM((16, 32, 128), F32),
                pltpu.VMEM((ns + 1, 16, 128), BF16),
                pltpu.VMEM((ns, 2, 16, 128), BF16),
                pltpu.VMEM((ns, 16, 128), BF16),
                pltpu.VMEM((2, 3, 40, 16), F32),
                pltpu.VMEM((2, 2, 48, 128), F32),
                pltpu.VMEM((2, 16, 128), F32),
                pltpu.VMEM((256, 256), BF16),
                pltpu.VMEM((8, 256), F32),
                pltpu.VMEM((8, 256), BF16),
                pltpu.VMEM((ns, 8, 256), BF16),
                pltpu.VMEM((192, 8 * ns), BF16),
                dma, dma((5,)), dma((14,)), dma((14,)), dma((2,)), dma((2,)), dma, dma, dma, dma, dma, dma,
            ],
            compiler_params=pltpu.CompilerParams(
                collective_id=0, has_side_effects=True, vmem_limit_bytes=40 * 2**20),
        )(*[pltpu.with_memory_space_constraint(x, pltpu.HBM) for x in (
            by_tap(first_kernel), by_tap(second_kernel), density_weight, upsample_kernel, color_weight.T, volume)])
        return out

    placed = (P(None, "slab", "tile", None), P(), P(), P(), P(), P())
    return jax.shard_map(
        body, mesh=mesh, in_specs=placed, out_specs=P(None, "tile", None), check_vma=False
    )
```

```python
import jax
import jax.numpy as jnp
from jax import lax
from jax.experimental import pallas as pl
from jax.experimental.pallas import tpu as pltpu
from jax.sharding import PartitionSpec as P

MESH = pl.DeviceIdType.MESH
F32 = jnp.float32
BF16 = jnp.bfloat16


def gelu(x):
    inner = x * (0.7978845608028654 + (0.7978845608028654 * 0.044715) * (x * x))
    half = 0.5 * x
    return half * jnp.tanh(inner) + half


def gelu_of_half(y):
    inner = y * (2 * 0.7978845608028654 + (8 * 0.7978845608028654 * 0.044715) * (y * y))
    return y * jnp.tanh(inner) + y


def contract(a, b):
    return lax.dot_general(a, b, (((0,), (0,)), ((), ())), preferred_element_type=F32)


def softplus(x):
    t = jnp.exp(-jnp.abs(x))
    tail = jnp.where(t < 1e-3, t * (1.0 - 0.5 * t), jnp.log(1.0 + t))
    return jnp.maximum(x, 0.0) + tail


def kernel(ns, nt, k1_any, k2_any, dw_any, up_any, col_any, vol_ref, out_ref,
           k1_ref, k2_ref, dw_ref, up_ref, col_ref, v_ref, f_ref, e_ref, rx_ref, hs_ref, xb_ref, hb_ref, w1f_ref, w1_ref, w2f_ref, w2_ref,
           y_ref, fe_ref, op_ref, sum_ref, tsf_ref, ts_ref, tr_ref, ti_ref, ea_ref, ps_ref, sb_ref, rb_ref, rb2_ref,
           ks_ref, base_ref, acc_ref, im_ref, gsf_ref, gs_ref, gb_ref, pm_ref,
           vol_sem, in_sem, hs_sem, hr_sem, ts_sem, t_sem, rs_sem, r_sem, r2_sem, r2s_sem, gs_sem, g_sem):
    slab = lax.axis_index("slab")
    tile = lax.axis_index("tile")
    up, down = lax.rem(slab + 1, ns), lax.rem(slab + ns - 1, ns)
    east, west = lax.rem(tile + 1, nt), lax.rem(tile + nt - 1, nt)

    own = pltpu.make_async_copy(vol_ref, v_ref.at[:, 4:12], vol_sem)
    own.start()

    barrier = pltpu.get_barrier_semaphore()

    def greet(s, t):
        pl.semaphore_signal(barrier, inc=1, device_id=(s, t), device_id_type=MESH)

    for t in (east, west):
        for s in (slab, up, down):
            greet(s, t)

    for d in range(1, ns):
        peer = slab + d
        greet(peer - jnp.where(peer >= ns, ns, 0), tile)

    @pl.when(slab == ns - 1)
    def _():
        @pl.loop(0, ns)
        def _(s):
            greet(s, east)

    params = [pltpu.make_async_copy(src, dst, in_sem.at[n]) for n, (src, dst) in enumerate(
        ((k1_any, k1_ref), (k2_any, k2_ref), (dw_any, dw_ref), (up_any, up_ref), (col_any, col_ref)))]
    for copy in params:
        copy.start()

    pl.semaphore_wait(barrier, (ns - 1) + 6 + 1)
    halos = []

    def send(src, dst, n, s, t):
        copy = pltpu.make_async_remote_copy(src_ref=src, dst_ref=dst, send_sem=hs_sem.at[n], recv_sem=hr_sem.at[n],
                                            device_id=(s, t), device_id_type=MESH)
        copy.start()
        halos.append(copy)

    for part in range(4):
        rows = slice(8 * part, 8 * part + 8)
        send(vol_ref.at[:, 5:8, rows], v_ref.at[:, 1:4, rows], 2 * part, up, tile)
        send(vol_ref.at[:, 0:3, rows], v_ref.at[:, 12:15, rows], 2 * part + 1, down, tile)

    own.wait()

    @pl.loop(0, 16)
    def _(c):
        f_ref[c, 0:32, :] = jnp.zeros((32, 128), F32)
        f_ref[c, 540:572, :] = jnp.zeros((32, 128), F32)
        f_ref[c, 144:176, :] = v_ref[c, 4].astype(F32)
        f_ref[c, 180:212, :] = v_ref[c, 5].astype(F32)
        f_ref[c, 216:248, :] = v_ref[c, 6].astype(F32)
        f_ref[c, 252:284, :] = v_ref[c, 7].astype(F32)
        f_ref[c, 288:320, :] = v_ref[c, 8].astype(F32)
        f_ref[c, 324:356, :] = v_ref[c, 9].astype(F32)
        f_ref[c, 360:392, :] = v_ref[c, 10].astype(F32)
        f_ref[c, 396:428, :] = v_ref[c, 11].astype(F32)
        for side in range(2):
            for k in range(3):
                h = 29 * side + k
                for zh in range(2):
                    e_ref[side, zh, c * 3 + k] = f_ref[c, pl.ds((4 + 4 * zh) * 36 + h, 4, stride=36), :].astype(BF16)

    send(e_ref.at[1], rx_ref.at[0, 1:3], 8, slab, east)
    send(e_ref.at[0], rx_ref.at[1, 1:3], 9, slab, west)
    send(e_ref.at[1, 1], rx_ref.at[0, 0], 10, up, east)
    send(e_ref.at[1, 0], rx_ref.at[0, 3], 11, down, east)
    send(e_ref.at[0, 1], rx_ref.at[1, 0], 12, up, west)
    send(e_ref.at[0, 0], rx_ref.at[1, 3], 13, down, west)

    row = lax.broadcasted_iota(jnp.int32, (24, 128), 0)
    lane = lax.broadcasted_iota(jnp.int32, (24, 128), 1)
    z_out = lax.rem(row, 12) + 2
    z_in = lax.rem(lane, 16)
    first = slab * 8 - 4
    keep = (z_out + first >= 0) & (z_out + first < 8 * ns)
    keep = keep & (z_in + first >= 0) & (z_in + first < 8 * ns)

    for copy in params:
        copy.wait()
    ks_ref[...] = jnp.zeros((2, 3, 40, 16), F32)
    prow = lax.broadcasted_iota(jnp.int32, (40, 128), 0)
    plane = lax.broadcasted_iota(jnp.int32, (40, 128), 1)
    pi, pa, pb = lax.rem(prow, 4), prow // 12, lax.rem(prow // 4, 3)
    for conv, k_ref in enumerate((k1_ref, k2_ref)):
        for c in range(3):
            for ab in range(9):
                ks_ref[conv, c, 4 * ab:4 * ab + 4, :] = k_ref[ab * 3 + c].astype(F32)
        spot = lax.rem(lax.rem(pi, 2) * 64 + pb * 16 + pa * (1 + conv), 128)
        for half in range(2):
            place = jnp.where((spot == plane) & (pi // 2 == half) & (prow < 36), 0.5 if conv == 0 else 1.0, 0.0).astype(BF16)
            for c in range(3):
                base_ref[conv, half, 16 * c:16 * c + 16, :] = contract(ks_ref[conv, c].astype(BF16), place)

    @pl.loop(0, 12)
    def _(gc):
        g, c = gc // 3, lax.rem(gc, 3)
        for o in range(4):
            for half in range(2):
                line = base_ref[0, half, pl.ds(c * 16 + g * 4 + o, 1), :]
                line = jnp.broadcast_to(line, (24, 128))
                band = jnp.where(row < 12, pltpu.roll(line, 1, 1, stride=1, stride_axis=0),
                                 pltpu.roll(line, 5, 1, stride=1, stride_axis=0))
                w1f_ref[g, half, pl.ds(pl.multiple_of(o * 72 + c * 24, 8), 24), :] = jnp.where(keep, band, 0.0)
                line = base_ref[1, half, pl.ds(c * 16 + g * 4 + o, 1), :]
                for hh in range(2):
                    band = pltpu.roll(jnp.broadcast_to(line, (8, 128)), hh * 16, 1, stride=1, stride_axis=0)
                    w2f_ref[g, half, pl.ds(c * 8 + o * 2 + hh, 8, stride=24), :] = band

    for half in range(2):
        w1_ref[:, :, half * 128:half * 128 + 128] = w1f_ref[:, half].astype(BF16)
        w2_ref[:, :, half * 128:half * 128 + 128] = w2f_ref[:, half].astype(BF16)

    irow = lax.broadcasted_iota(jnp.int32, (256, 256), 0)
    icol = lax.broadcasted_iota(jnp.int32, (256, 256), 1)
    im_ref[...] = jnp.where(icol == 2 * lax.rem(irow, 128) + irow // 128, 1.0, 0.0).astype(BF16)
    prow = lax.broadcasted_iota(jnp.int32, (192, 256), 0)
    pcol = lax.broadcasted_iota(jnp.int32, (192, 256), 1)
    source = lax.rem(prow, 64) // 2 * 8 + lax.rem(prow, 2) * 4 + prow // 64
    pm_ref[...] = jnp.where(pcol == source, 1.0, 0.0).astype(BF16)

    inside = (tile > 0, tile < nt - 1)

    sub = lax.broadcasted_iota(jnp.int32, (8, 128), 0)
    chan = sub // 2
    dwv = []
    for g in range(4):
        v = jnp.where(chan == 0, dw_ref[4 * g], 0.0)
        for o in range(1, 4):
            v = jnp.where(chan == o, dw_ref[4 * g + o], v)
        dwv.append(v)
    wlane = lax.broadcasted_iota(jnp.int32, (24, 128), 1)
    wlane2 = lax.broadcasted_iota(jnp.int32, (8, 128), 1)

    def relayout(part):
        halos[2 * part].wait()
        halos[2 * part + 1].wait()

        @pl.loop(0, 16)
        def _(c):
            for z in (1, 2, 3, 12, 13, 14):
                f_ref[c, 36 * z + 8 * part:36 * z + 8 * part + 8, :] = v_ref[c, z, 8 * part:8 * part + 8].astype(F32)
            for h in range(8 * part, 8 * part + 8):
                xb_ref[c, h + 3] = f_ref[c, pl.ds(h, 16, stride=36), :].astype(BF16)

    pending = []
    turns = [0]

    def issue(matrix, data, finish):
        rows = matrix.shape[0]
        place = y_ref.at[turns[0], 0:rows]
        turns[0] = 1 - turns[0]
        place[...] = jnp.dot(matrix, data, preferred_element_type=F32)
        flush()
        pending.append(lambda: finish(place))

    def flush():
        while pending:
            pending.pop()()

    def first_conv(j):
        for g in range(4):
            data = jnp.concatenate(
                [xb_ref[4 * g:4 * g + 4, 4 * j + 2 * n:4 * j + 2 * n + 4].reshape(256, 128) for n in range(2)], axis=1)

            def finish(y, g=g):
                for o in range(4):
                    for n in range(2):
                        cols = slice(n * 128, n * 128 + 128)
                        total = y[72 * o + 24:72 * o + 48, cols]
                        total = total + jnp.where(wlane == 0, 0.0, pltpu.roll(y[72 * o:72 * o + 24, cols], 1, 1))
                        total = total + jnp.where(wlane == 127, 0.0, pltpu.roll(y[72 * o + 48:72 * o + 72, cols], 127, 1))
                        total = gelu_of_half(total)
                        if (j, n) == (0, 0):
                            total = jnp.where(inside[0], total, 0.0)
                        if (j, n) == (8, 1):
                            total = jnp.where(inside[1], total, 0.0)
                        hb_ref[4 * g + o, 0, 2 * j + n] = total[0:16].astype(BF16)
                        hb_ref[4 * g + o, 1, 2 * j + n] = pltpu.roll(total, 12, 0)[0:16].astype(BF16)

            issue(w1_ref[g], data, finish)

    def second_conv(n):
        k = (n + 1) % 8
        for g in range(4):
            data = jnp.concatenate(
                [hb_ref[4 * g:4 * g + 4, p, 2 * k:2 * k + 4].reshape(256, 128) for p in range(2)], axis=1)

            def finish(y, g=g):
                for z in range(8):
                    for p in range(2):
                        cols = slice(p * 128, p * 128 + 128)
                        total = y[24 * z + 8:24 * z + 16, cols]
                        total = total + jnp.where(wlane2 < 2, 0.0, pltpu.roll(y[24 * z:24 * z + 8, cols], 2, 1))
                        total = total + jnp.where(wlane2 >= 126, 0.0, pltpu.roll(y[24 * z + 16:24 * z + 24, cols], 126, 1))
                        fe_ref[2 * n + p, g, z] = total
                if g == 3:
                    optics(n)

            issue(w2_ref[g], data, finish)

    def optics(n):
        for p in range(2):
            subtotal = jnp.zeros((8, 128), F32)
            for z in range(8):
                x = dwv[0] * fe_ref[2 * n + p, 0, z]
                for g in range(1, 4):
                    x = x + dwv[g] * fe_ref[2 * n + p, g, z]
                x = x + pltpu.roll(x, 4, 0)
                x = x + pltpu.roll(x, 2, 0)
                depth = (slab * 8 + z).astype(F32)
                optical = softplus(x) * (1.0 + 2.0 * depth / (8 * ns - 1))
                op_ref[2 * n + p, z] = optical
                subtotal = subtotal + optical
            sum_ref[2 * n + p] = subtotal

    def push(src, dst, sends, recv, peer):
        return pltpu.make_async_remote_copy(src_ref=src, dst_ref=dst, send_sem=sends, recv_sem=recv,
                                            device_id=(peer, tile), device_id_type=MESH)

    def to_all(src, dst, sends, recv):
        for d in range(1, ns):
            peer = slab + d
            push(src, dst.at[slab], sends, recv, peer - jnp.where(peer >= ns, ns, 0)).start()

    def from_all(dst, sends, recv):
        every = dst.at[pl.ds(0, ns - 1)]
        push(every, every, sends, recv, up).wait()

    def send_totals(half):
        for m in range(2):
            packed = sum_ref[8 * half + 4 * m]
            for q in range(1, 4):
                packed = jnp.where(chan == q, sum_ref[8 * half + 4 * m + q], packed)
            tsf_ref[half, 8 * m:8 * m + 8, :] = packed
        ts_ref[half] = tsf_ref[half].astype(BF16)
        tr_ref[half, slab] = tsf_ref[half].astype(BF16)
        to_all(ts_ref.at[half], tr_ref.at[half], ts_sem.at[half], t_sem.at[half])

    relayout(0)
    first_conv(1)
    relayout(1)
    first_conv(2)
    second_conv(0)
    first_conv(3)
    relayout(2)
    second_conv(1)
    first_conv(4)
    second_conv(2)
    first_conv(5)
    relayout(3)
    second_conv(3)
    first_conv(6)
    send_totals(0)
    second_conv(4)
    first_conv(7)

    for copy in halos[8:]:
        copy.wait()

    @pl.loop(0, 16)
    def _(c):
        for side in range(2):
            for k in range(3):
                for blk in range(4):
                    hs_ref[side, c * 3 + k, 4 * blk:4 * blk + 4, :] = rx_ref[side, blk, c * 3 + k].astype(F32)
                xb_ref[c, 35 * side + k] = jnp.where(inside[side], hs_ref[side, c * 3 + k], 0.0).astype(BF16)

    second_conv(5)
    first_conv(8)
    second_conv(6)
    first_conv(0)
    second_conv(7)
    flush()
    send_totals(1)

    def shade(half):
        from_all(tr_ref.at[half], ts_sem.at[half], t_sem.at[half])

        def gather(s, carry):
            total, earlier = carry
            x = tr_ref[half, s].astype(F32)
            return total + x, earlier + jnp.where(s < slab, x, 0.0)

        zero = jnp.zeros((16, 128), F32)
        total, earlier = lax.fori_loop(0, ns, gather, (zero, zero), unroll=8)
        ti_ref[...] = 1.0 / total
        ea_ref[...] = earlier

        @pl.loop(0, 2)
        def _(m):
            rows = pl.ds(pl.multiple_of(8 * m, 8), 8)
            inverse4, before4 = ti_ref[rows, :], ea_ref[rows, :]
            for q in range(4):
                wi = 8 * half + 4 * m + q

                def spread(v):
                    v = jnp.where(chan == q, v, 0.0)
                    v = v + pltpu.roll(v, 4, 0)
                    return v + pltpu.roll(v, 2, 0)

                inverse, before = spread(inverse4), spread(before4)
                through = jnp.exp(-before * inverse)
                sums = [jnp.zeros((8, 128), F32)] * 4
                for z in range(8):
                    before = before + op_ref[wi, z]
                    after = jnp.exp(-before * inverse)
                    weight = through - after
                    through = after
                    for g in range(4):
                        sums[g] = sums[g] + weight * fe_ref[wi, g, z]
                for g in range(4):
                    ps_ref[wi, 8 * g:8 * g + 8, :] = sums[g]
                k = lax.rem(4 * half + 2 * m + q // 2 + 1, 8)
                for hh in range(2):
                    sb_ref[4 * k + 2 * hh + q % 2] = ps_ref[wi, pl.ds(hh, 16, stride=2), :].astype(BF16)

    def send_rows(owner):
        @pl.when(owner != slab)
        def _():
            push(sb_ref.at[pl.ds(owner, 2)], rb_ref.at[slab], rs_sem, r_sem, owner).start()

    sb_ref[32] = jnp.zeros((16, 128), BF16)
    shade(0)

    turn = lax.rem(slab, 15)
    for e in range(15):
        at = turn + e
        send_rows(at - jnp.where(at >= 15, 15, 0) + 4)

    shade(1)
    below = pltpu.make_async_remote_copy(src_ref=sb_ref.at[0], dst_ref=rb2_ref.at[slab], send_sem=r2s_sem,
                                         recv_sem=r2_sem, device_id=(ns - 1, west), device_id_type=MESH)
    below.start()

    turn = lax.rem(slab, 17)
    for e in range(17):
        at = turn + e
        at = at - jnp.where(at >= 17, 17, 0)
        send_rows(at + jnp.where(at >= 4, 15, 0))

    rb_ref[slab] = sb_ref[pl.ds(slab, 2)]
    from_all(rb_ref, rs_sem, r_sem)
    below.wait_send()

    def collect(s, carry):
        return carry + rb_ref[s].astype(F32)

    acc_ref[...] = lax.fori_loop(0, ns, collect, jnp.zeros((2, 16, 128), F32), unroll=8)

    @pl.when(slab == ns - 1)
    def _():
        pltpu.make_async_remote_copy(src_ref=rb2_ref, dst_ref=rb2_ref, send_sem=r2s_sem, recv_sem=r2_sem,
                                     device_id=(ns - 1, west), device_id_type=MESH).wait_recv()

        def collect2(s, carry):
            return carry + rb2_ref[s].astype(F32)

        below_row = lax.fori_loop(0, ns, collect2, jnp.zeros((16, 128), F32), unroll=8)
        acc_ref[1] = jnp.where(tile < nt - 1, below_row, 0.0)

    lane16 = lax.broadcasted_iota(jnp.int32, (16, 128), 1)
    shaded = []
    for r in range(2):
        s = acc_ref[r].astype(BF16)
        s32 = s.astype(F32)
        right = jnp.where(lane16 == 127, 0.0, pltpu.roll(s32, 127, 1)).astype(BF16)
        shaded.append((s, right))

    taps = (((1, 0),), ((0, 1), (2, 0)))
    gsf_ref[...] = jnp.zeros((8, 256), F32)
    for a in range(2):
        pair = []
        for b in range(2):
            y = jnp.zeros((16, 128), F32)
            for r, p in taps[a]:
                for s, q in taps[b]:
                    y = y + contract(up_ref[r, s], shaded[p][q])
            hidden = gelu(y).astype(BF16)
            pair.append(jnp.dot(col_ref[...], hidden, preferred_element_type=F32).astype(BF16))
        line = jnp.dot(jnp.concatenate(pair, axis=1), im_ref[...], preferred_element_type=F32)
        gsf_ref[4 * a:4 * a + 3, :] = line
    gs_ref[...] = gsf_ref[...].astype(BF16)
    gb_ref[slab] = gsf_ref[...].astype(BF16)

    to_all(gs_ref, gb_ref, gs_sem, g_sem)
    from_all(gb_ref, gs_sem, g_sem)

    rows = jnp.concatenate([gb_ref[k] for k in range(ns)], axis=0)
    lines = jnp.dot(pm_ref[...], rows, preferred_element_type=F32)
    for color in range(3):
        out_ref[color] = lines[64 * color:64 * color + 64]


def by_tap(kern):
    return kern.transpose(2, 3, 4, 1, 0).reshape(27, 4, 16)


def solution(mesh):
    ns, nt = mesh.shape["slab"], mesh.shape["tile"]

    def body(volume, first_kernel, second_kernel, density_weight, upsample_kernel, color_weight):
        vmem = pl.BlockSpec(memory_space=pltpu.VMEM)
        dma = pltpu.SemaphoreType.DMA
        out = pl.pallas_call(
            lambda *refs: kernel(ns, nt, *refs),
            out_shape=jax.ShapeDtypeStruct((3, 64, 256), F32),
            in_specs=[pl.BlockSpec(memory_space=pltpu.HBM)] * 6,
            out_specs=vmem,
            scratch_shapes=[
                pltpu.VMEM((27, 4, 16), BF16),
                pltpu.VMEM((27, 4, 16), BF16),
                pltpu.SMEM((16,), F32),
                pltpu.VMEM((3, 3, 16, 16), BF16),
                pltpu.VMEM((3, 16), BF16),
                pltpu.VMEM((16, 16, 32, 128), BF16),
                pltpu.VMEM((16, 576, 128), F32),
                pltpu.VMEM((2, 2, 48, 4, 128), BF16),
                pltpu.VMEM((2, 4, 48, 4, 128), BF16),
                pltpu.VMEM((2, 48, 16, 128), F32),
                pltpu.VMEM((16, 38, 16, 128), BF16),
                pltpu.VMEM((16, 2, 18, 16, 128), BF16),
                pltpu.VMEM((4, 2, 288, 128), F32),
                pltpu.VMEM((4, 288, 256), BF16),
                pltpu.VMEM((4, 2, 192, 128), F32),
                pltpu.VMEM((4, 192, 256), BF16),
                pltpu.VMEM((2, 288, 256), F32),
                pltpu.VMEM((16, 4, 8, 8, 128), F32),
                pltpu.VMEM((16, 8, 8, 128), F32),
                pltpu.VMEM((16, 8, 128), F32),
                pltpu.VMEM((2, 16, 128), F32),
                pltpu.VMEM((2, 16, 128), BF16),
                pltpu.VMEM((2, ns, 16, 128), BF16),
                pltpu.VMEM((16, 128), F32),
                pltpu.VMEM((16, 128), F32),
                pltpu.VMEM((16, 32, 128), F32),
                pltpu.VMEM((ns + 1, 16, 128), BF16),
                pltpu.VMEM((ns, 2, 16, 128), BF16),
                pltpu.VMEM((ns, 16, 128), BF16),
                pltpu.VMEM((2, 3, 40, 16), F32),
                pltpu.VMEM((2, 2, 48, 128), F32),
                pltpu.VMEM((2, 16, 128), F32),
                pltpu.VMEM((256, 256), BF16),
                pltpu.VMEM((8, 256), F32),
                pltpu.VMEM((8, 256), BF16),
                pltpu.VMEM((ns, 8, 256), BF16),
                pltpu.VMEM((192, 8 * ns), BF16),
                dma, dma((5,)), dma((14,)), dma((14,)), dma((2,)), dma((2,)), dma, dma, dma, dma, dma, dma,
            ],
            compiler_params=pltpu.CompilerParams(
                collective_id=0, has_side_effects=True, vmem_limit_bytes=40 * 2**20),
        )(*[pltpu.with_memory_space_constraint(x, pltpu.HBM) for x in (
            by_tap(first_kernel), by_tap(second_kernel), density_weight, upsample_kernel, color_weight.T, volume)])
        return out

    placed = (P(None, "slab", "tile", None), P(), P(), P(), P(), P())
    return jax.shard_map(
        body, mesh=mesh, in_specs=placed, out_specs=P(None, "tile", None), check_vma=False
    )
```

```python
import jax
import jax.numpy as jnp
from jax import lax
from jax.experimental import pallas as pl
from jax.experimental.pallas import tpu as pltpu
from jax.sharding import PartitionSpec as P

MESH = pl.DeviceIdType.MESH
F32 = jnp.float32
BF16 = jnp.bfloat16


def gelu(x):
    inner = x * (0.7978845608028654 + (0.7978845608028654 * 0.044715) * (x * x))
    half = 0.5 * x
    return half * jnp.tanh(inner) + half


def gelu_of_half(y):
    inner = y * (2 * 0.7978845608028654 + (8 * 0.7978845608028654 * 0.044715) * (y * y))
    return y * jnp.tanh(inner) + y


def contract(a, b):
    return lax.dot_general(a, b, (((0,), (0,)), ((), ())), preferred_element_type=F32)


def softplus(x):
    t = jnp.exp(-jnp.abs(x))
    tail = jnp.where(t < 1e-3, t * (1.0 - 0.5 * t), jnp.log(1.0 + t))
    return jnp.maximum(x, 0.0) + tail


def kernel(ns, nt, k1_any, k2_any, dw_any, up_any, col_any, vol_ref, out_ref,
           k1_ref, k2_ref, dw_ref, up_ref, col_ref, v_ref, f_ref, e_ref, rx_ref, hs_ref, xb_ref, hb_ref, w1f_ref, w1_ref, w2f_ref, w2_ref,
           y_ref, fe_ref, op_ref, sum_ref, tsf_ref, ts_ref, tr_ref, ti_ref, ea_ref, ps_ref, sb_ref, rb_ref, rb2_ref,
           ks_ref, base_ref, acc_ref, im_ref, gsf_ref, gs_ref, gb_ref, pm_ref,
           vol_sem, in_sem, hs_sem, hr_sem, ts_sem, t_sem, rs_sem, r_sem, r2_sem, r2s_sem, gs_sem, g_sem):
    slab = lax.axis_index("slab")
    tile = lax.axis_index("tile")
    up, down = lax.rem(slab + 1, ns), lax.rem(slab + ns - 1, ns)
    east, west = lax.rem(tile + 1, nt), lax.rem(tile + nt - 1, nt)

    own = pltpu.make_async_copy(vol_ref, v_ref.at[:, 4:12], vol_sem)
    own.start()

    barrier = pltpu.get_barrier_semaphore()

    def greet(s, t):
        pl.semaphore_signal(barrier, inc=1, device_id=(s, t), device_id_type=MESH)

    for t in (east, west):
        for s in (slab, up, down):
            greet(s, t)

    for d in range(1, ns):
        peer = slab + d
        greet(peer - jnp.where(peer >= ns, ns, 0), tile)

    @pl.when(slab == ns - 1)
    def _():
        @pl.loop(0, ns)
        def _(s):
            greet(s, east)

    params = [pltpu.make_async_copy(src, dst, in_sem.at[n]) for n, (src, dst) in enumerate(
        ((k1_any, k1_ref), (k2_any, k2_ref), (dw_any, dw_ref), (up_any, up_ref), (col_any, col_ref)))]
    for copy in params:
        copy.start()

    pl.semaphore_wait(barrier, (ns - 1) + 6 + 1)
    halos = [None] * 14

    def send(src, dst, n, s, t):
        copy = pltpu.make_async_remote_copy(src_ref=src, dst_ref=dst, send_sem=hs_sem.at[n], recv_sem=hr_sem.at[n],
                                            device_id=(s, t), device_id_type=MESH)
        copy.start()
        halos[n] = copy

    def send_layers(part):
        rows = slice(8 * part, 8 * part + 8)
        send(vol_ref.at[:, 5:8, rows], v_ref.at[:, 1:4, rows], 2 * part, up, tile)
        send(vol_ref.at[:, 0:3, rows], v_ref.at[:, 12:15, rows], 2 * part + 1, down, tile)

    send_layers(0)
    send_layers(1)
    send_layers(2)

    own.wait()

    @pl.loop(0, 16)
    def _(c):
        f_ref[c, 0:32, :] = jnp.zeros((32, 128), F32)
        f_ref[c, 540:572, :] = jnp.zeros((32, 128), F32)
        f_ref[c, 144:176, :] = v_ref[c, 4].astype(F32)
        f_ref[c, 180:212, :] = v_ref[c, 5].astype(F32)
        f_ref[c, 216:248, :] = v_ref[c, 6].astype(F32)
        f_ref[c, 252:284, :] = v_ref[c, 7].astype(F32)
        f_ref[c, 288:320, :] = v_ref[c, 8].astype(F32)
        f_ref[c, 324:356, :] = v_ref[c, 9].astype(F32)
        f_ref[c, 360:392, :] = v_ref[c, 10].astype(F32)
        f_ref[c, 396:428, :] = v_ref[c, 11].astype(F32)
        for side in range(2):
            for k in range(3):
                h = 29 * side + k
                for zh in range(2):
                    e_ref[side, zh, c * 3 + k] = f_ref[c, pl.ds((4 + 4 * zh) * 36 + h, 4, stride=36), :].astype(BF16)

    send(e_ref.at[1], rx_ref.at[0, 1:3], 8, slab, east)
    send(e_ref.at[0], rx_ref.at[1, 1:3], 9, slab, west)
    send_layers(3)
    send(e_ref.at[1, 1], rx_ref.at[0, 0], 10, up, east)
    send(e_ref.at[1, 0], rx_ref.at[0, 3], 11, down, east)
    send(e_ref.at[0, 1], rx_ref.at[1, 0], 12, up, west)
    send(e_ref.at[0, 0], rx_ref.at[1, 3], 13, down, west)

    row = lax.broadcasted_iota(jnp.int32, (24, 128), 0)
    lane = lax.broadcasted_iota(jnp.int32, (24, 128), 1)
    z_out = lax.rem(row, 12) + 2
    z_in = lax.rem(lane, 16)
    first = slab * 8 - 4
    keep = (z_out + first >= 0) & (z_out + first < 8 * ns)
    keep = keep & (z_in + first >= 0) & (z_in + first < 8 * ns)

    for copy in params:
        copy.wait()
    ks_ref[...] = jnp.zeros((2, 3, 40, 16), F32)
    prow = lax.broadcasted_iota(jnp.int32, (40, 128), 0)
    plane = lax.broadcasted_iota(jnp.int32, (40, 128), 1)
    pi, pa, pb = lax.rem(prow, 4), prow // 12, lax.rem(prow // 4, 3)
    for conv, k_ref in enumerate((k1_ref, k2_ref)):
        for c in range(3):
            for ab in range(9):
                ks_ref[conv, c, 4 * ab:4 * ab + 4, :] = k_ref[ab * 3 + c].astype(F32)
        spot = lax.rem(lax.rem(pi, 2) * 64 + pb * 16 + pa * (1 + conv), 128)
        for half in range(2):
            place = jnp.where((spot == plane) & (pi // 2 == half) & (prow < 36), 0.5 if conv == 0 else 1.0, 0.0).astype(BF16)
            for c in range(3):
                base_ref[conv, half, 16 * c:16 * c + 16, :] = contract(ks_ref[conv, c].astype(BF16), place)

    @pl.loop(0, 12)
    def _(gc):
        g, c = gc // 3, lax.rem(gc, 3)
        for o in range(4):
            for half in range(2):
                line = base_ref[0, half, pl.ds(c * 16 + g * 4 + o, 1), :]
                line = jnp.broadcast_to(line, (24, 128))
                band = jnp.where(row < 12, pltpu.roll(line, 1, 1, stride=1, stride_axis=0),
                                 pltpu.roll(line, 5, 1, stride=1, stride_axis=0))
                w1f_ref[g, half, pl.ds(pl.multiple_of(o * 72 + c * 24, 8), 24), :] = jnp.where(keep, band, 0.0)
                line = base_ref[1, half, pl.ds(c * 16 + g * 4 + o, 1), :]
                for hh in range(2):
                    band = pltpu.roll(jnp.broadcast_to(line, (8, 128)), hh * 16, 1, stride=1, stride_axis=0)
                    w2f_ref[g, half, pl.ds(c * 8 + o * 2 + hh, 8, stride=24), :] = band

    for half in range(2):
        w1_ref[:, :, half * 128:half * 128 + 128] = w1f_ref[:, half].astype(BF16)
        w2_ref[:, :, half * 128:half * 128 + 128] = w2f_ref[:, half].astype(BF16)

    irow = lax.broadcasted_iota(jnp.int32, (256, 256), 0)
    icol = lax.broadcasted_iota(jnp.int32, (256, 256), 1)
    im_ref[...] = jnp.where(icol == 2 * lax.rem(irow, 128) + irow // 128, 1.0, 0.0).astype(BF16)
    prow = lax.broadcasted_iota(jnp.int32, (192, 256), 0)
    pcol = lax.broadcasted_iota(jnp.int32, (192, 256), 1)
    source = lax.rem(prow, 64) // 2 * 8 + lax.rem(prow, 2) * 4 + prow // 64
    pm_ref[...] = jnp.where(pcol == source, 1.0, 0.0).astype(BF16)

    inside = (tile > 0, tile < nt - 1)

    sub = lax.broadcasted_iota(jnp.int32, (8, 128), 0)
    chan = sub // 2
    dwv = []
    for g in range(4):
        v = jnp.where(chan == 0, dw_ref[4 * g], 0.0)
        for o in range(1, 4):
            v = jnp.where(chan == o, dw_ref[4 * g + o], v)
        dwv.append(v)
    wlane = lax.broadcasted_iota(jnp.int32, (24, 128), 1)
    wlane2 = lax.broadcasted_iota(jnp.int32, (8, 128), 1)

    def relayout(part):
        halos[2 * part].wait()
        halos[2 * part + 1].wait()

        @pl.loop(0, 16)
        def _(c):
            for z in (1, 2, 3, 12, 13, 14):
                f_ref[c, 36 * z + 8 * part:36 * z + 8 * part + 8, :] = v_ref[c, z, 8 * part:8 * part + 8].astype(F32)
            for h in range(8 * part, 8 * part + 8):
                xb_ref[c, h + 3] = f_ref[c, pl.ds(h, 16, stride=36), :].astype(BF16)

    pending = []
    turns = [0]

    def issue(matrix, data, finish):
        rows = matrix.shape[0]
        place = y_ref.at[turns[0], 0:rows]
        turns[0] = 1 - turns[0]
        place[...] = jnp.dot(matrix, data, preferred_element_type=F32)
        flush()
        pending.append(lambda: finish(place))

    def flush():
        while pending:
            pending.pop()()

    def first_conv(j):
        for g in range(4):
            data = jnp.concatenate(
                [xb_ref[4 * g:4 * g + 4, 4 * j + 2 * n:4 * j + 2 * n + 4].reshape(256, 128) for n in range(2)], axis=1)

            def finish(y, g=g):
                for o in range(4):
                    for n in range(2):
                        cols = slice(n * 128, n * 128 + 128)
                        total = y[72 * o + 24:72 * o + 48, cols]
                        total = total + jnp.where(wlane == 0, 0.0, pltpu.roll(y[72 * o:72 * o + 24, cols], 1, 1))
                        total = total + jnp.where(wlane == 127, 0.0, pltpu.roll(y[72 * o + 48:72 * o + 72, cols], 127, 1))
                        total = gelu_of_half(total)
                        if (j, n) == (0, 0):
                            total = jnp.where(inside[0], total, 0.0)
                        if (j, n) == (8, 1):
                            total = jnp.where(inside[1], total, 0.0)
                        hb_ref[4 * g + o, 0, 2 * j + n] = total[0:16].astype(BF16)
                        hb_ref[4 * g + o, 1, 2 * j + n] = pltpu.roll(total, 12, 0)[0:16].astype(BF16)

            issue(w1_ref[g], data, finish)

    def second_conv(n):
        k = (n + 1) % 8
        for g in range(4):
            data = jnp.concatenate(
                [hb_ref[4 * g:4 * g + 4, p, 2 * k:2 * k + 4].reshape(256, 128) for p in range(2)], axis=1)

            def finish(y, g=g):
                for z in range(8):
                    for p in range(2):
                        cols = slice(p * 128, p * 128 + 128)
                        total = y[24 * z + 8:24 * z + 16, cols]
                        total = total + jnp.where(wlane2 < 2, 0.0, pltpu.roll(y[24 * z:24 * z + 8, cols], 2, 1))
                        total = total + jnp.where(wlane2 >= 126, 0.0, pltpu.roll(y[24 * z + 16:24 * z + 24, cols], 126, 1))
                        fe_ref[2 * n + p, g, z] = total
                if g == 3:
                    optics(n)

            issue(w2_ref[g], data, finish)

    def optics(n):
        for p in range(2):
            subtotal = jnp.zeros((8, 128), F32)
            for z in range(8):
                x = dwv[0] * fe_ref[2 * n + p, 0, z]
                for g in range(1, 4):
                    x = x + dwv[g] * fe_ref[2 * n + p, g, z]
                x = x + pltpu.roll(x, 4, 0)
                x = x + pltpu.roll(x, 2, 0)
                depth = (slab * 8 + z).astype(F32)
                optical = softplus(x) * (1.0 + 2.0 * depth / (8 * ns - 1))
                op_ref[2 * n + p, z] = optical
                subtotal = subtotal + optical
            sum_ref[2 * n + p] = subtotal

    def push(src, dst, sends, recv, peer):
        return pltpu.make_async_remote_copy(src_ref=src, dst_ref=dst, send_sem=sends, recv_sem=recv,
                                            device_id=(peer, tile), device_id_type=MESH)

    def to_all(src, dst, sends, recv):
        for d in range(1, ns):
            peer = slab + d
            push(src, dst.at[slab], sends, recv, peer - jnp.where(peer >= ns, ns, 0)).start()

    def from_all(dst, sends, recv):
        every = dst.at[pl.ds(0, ns - 1)]
        push(every, every, sends, recv, up).wait()

    def send_totals(half):
        for m in range(2):
            packed = sum_ref[8 * half + 4 * m]
            for q in range(1, 4):
                packed = jnp.where(chan == q, sum_ref[8 * half + 4 * m + q], packed)
            tsf_ref[half, 8 * m:8 * m + 8, :] = packed
        ts_ref[half] = tsf_ref[half].astype(BF16)
        tr_ref[half, slab] = tsf_ref[half].astype(BF16)
        to_all(ts_ref.at[half], tr_ref.at[half], ts_sem.at[half], t_sem.at[half])

    relayout(0)
    first_conv(1)
    relayout(1)
    first_conv(2)
    second_conv(0)
    first_conv(3)
    relayout(2)
    second_conv(1)
    first_conv(4)
    second_conv(2)
    first_conv(5)
    relayout(3)
    second_conv(3)
    first_conv(6)
    send_totals(0)
    second_conv(4)
    first_conv(7)

    for copy in halos[8:]:
        copy.wait()

    @pl.loop(0, 16)
    def _(c):
        for side in range(2):
            for k in range(3):
                for blk in range(4):
                    hs_ref[side, c * 3 + k, 4 * blk:4 * blk + 4, :] = rx_ref[side, blk, c * 3 + k].astype(F32)
                xb_ref[c, 35 * side + k] = jnp.where(inside[side], hs_ref[side, c * 3 + k], 0.0).astype(BF16)

    second_conv(5)
    first_conv(8)
    second_conv(6)
    first_conv(0)
    second_conv(7)
    flush()
    send_totals(1)

    def shade(half):
        from_all(tr_ref.at[half], ts_sem.at[half], t_sem.at[half])

        def gather(s, carry):
            total, earlier = carry
            x = tr_ref[half, s].astype(F32)
            return total + x, earlier + jnp.where(s < slab, x, 0.0)

        zero = jnp.zeros((16, 128), F32)
        total, earlier = lax.fori_loop(0, ns, gather, (zero, zero), unroll=8)
        ti_ref[...] = 1.0 / total
        ea_ref[...] = earlier

        @pl.loop(0, 2)
        def _(m):
            rows = pl.ds(pl.multiple_of(8 * m, 8), 8)
            inverse4, before4 = ti_ref[rows, :], ea_ref[rows, :]
            for q in range(4):
                wi = 8 * half + 4 * m + q

                def spread(v):
                    v = jnp.where(chan == q, v, 0.0)
                    v = v + pltpu.roll(v, 4, 0)
                    return v + pltpu.roll(v, 2, 0)

                inverse, before = spread(inverse4), spread(before4)
                through = jnp.exp(-before * inverse)
                sums = [jnp.zeros((8, 128), F32)] * 4
                for z in range(8):
                    before = before + op_ref[wi, z]
                    after = jnp.exp(-before * inverse)
                    weight = through - after
                    through = after
                    for g in range(4):
                        sums[g] = sums[g] + weight * fe_ref[wi, g, z]
                for g in range(4):
                    ps_ref[wi, 8 * g:8 * g + 8, :] = sums[g]
                k = lax.rem(4 * half + 2 * m + q // 2 + 1, 8)
                for hh in range(2):
                    sb_ref[4 * k + 2 * hh + q % 2] = ps_ref[wi, pl.ds(hh, 16, stride=2), :].astype(BF16)

    def send_rows(owner):
        @pl.when(owner != slab)
        def _():
            push(sb_ref.at[pl.ds(owner, 2)], rb_ref.at[slab], rs_sem, r_sem, owner).start()

    sb_ref[32] = jnp.zeros((16, 128), BF16)
    shade(0)

    turn = lax.rem(slab, 15)
    for e in range(15):
        at = turn + e
        send_rows(at - jnp.where(at >= 15, 15, 0) + 4)

    shade(1)
    below = pltpu.make_async_remote_copy(src_ref=sb_ref.at[0], dst_ref=rb2_ref.at[slab], send_sem=r2s_sem,
                                         recv_sem=r2_sem, device_id=(ns - 1, west), device_id_type=MESH)
    below.start()

    turn = lax.rem(slab, 17)
    for e in range(17):
        at = turn + e
        at = at - jnp.where(at >= 17, 17, 0)
        send_rows(at + jnp.where(at >= 4, 15, 0))

    rb_ref[slab] = sb_ref[pl.ds(slab, 2)]
    from_all(rb_ref, rs_sem, r_sem)
    below.wait_send()

    def collect(s, carry):
        return carry + rb_ref[s].astype(F32)

    acc_ref[...] = lax.fori_loop(0, ns, collect, jnp.zeros((2, 16, 128), F32), unroll=8)

    @pl.when(slab == ns - 1)
    def _():
        pltpu.make_async_remote_copy(src_ref=rb2_ref, dst_ref=rb2_ref, send_sem=r2s_sem, recv_sem=r2_sem,
                                     device_id=(ns - 1, west), device_id_type=MESH).wait_recv()

        def collect2(s, carry):
            return carry + rb2_ref[s].astype(F32)

        below_row = lax.fori_loop(0, ns, collect2, jnp.zeros((16, 128), F32), unroll=8)
        acc_ref[1] = jnp.where(tile < nt - 1, below_row, 0.0)

    lane16 = lax.broadcasted_iota(jnp.int32, (16, 128), 1)
    shaded = []
    for r in range(2):
        s = acc_ref[r].astype(BF16)
        s32 = s.astype(F32)
        right = jnp.where(lane16 == 127, 0.0, pltpu.roll(s32, 127, 1)).astype(BF16)
        shaded.append((s, right))

    taps = (((1, 0),), ((0, 1), (2, 0)))
    gsf_ref[...] = jnp.zeros((8, 256), F32)
    for a in range(2):
        pair = []
        for b in range(2):
            y = jnp.zeros((16, 128), F32)
            for r, p in taps[a]:
                for s, q in taps[b]:
                    y = y + contract(up_ref[r, s], shaded[p][q])
            hidden = gelu(y).astype(BF16)
            pair.append(jnp.dot(col_ref[...], hidden, preferred_element_type=F32).astype(BF16))
        line = jnp.dot(jnp.concatenate(pair, axis=1), im_ref[...], preferred_element_type=F32)
        gsf_ref[4 * a:4 * a + 3, :] = line
    gs_ref[...] = gsf_ref[...].astype(BF16)
    gb_ref[slab] = gsf_ref[...].astype(BF16)

    to_all(gs_ref, gb_ref, gs_sem, g_sem)
    from_all(gb_ref, gs_sem, g_sem)

    rows = jnp.concatenate([gb_ref[k] for k in range(ns)], axis=0)
    lines = jnp.dot(pm_ref[...], rows, preferred_element_type=F32)
    for color in range(3):
        out_ref[color] = lines[64 * color:64 * color + 64]


def by_tap(kern):
    return kern.transpose(2, 3, 4, 1, 0).reshape(27, 4, 16)


def solution(mesh):
    ns, nt = mesh.shape["slab"], mesh.shape["tile"]

    def body(volume, first_kernel, second_kernel, density_weight, upsample_kernel, color_weight):
        vmem = pl.BlockSpec(memory_space=pltpu.VMEM)
        dma = pltpu.SemaphoreType.DMA
        out = pl.pallas_call(
            lambda *refs: kernel(ns, nt, *refs),
            out_shape=jax.ShapeDtypeStruct((3, 64, 256), F32),
            in_specs=[pl.BlockSpec(memory_space=pltpu.HBM)] * 6,
            out_specs=vmem,
            scratch_shapes=[
                pltpu.VMEM((27, 4, 16), BF16),
                pltpu.VMEM((27, 4, 16), BF16),
                pltpu.SMEM((16,), F32),
                pltpu.VMEM((3, 3, 16, 16), BF16),
                pltpu.VMEM((3, 16), BF16),
                pltpu.VMEM((16, 16, 32, 128), BF16),
                pltpu.VMEM((16, 576, 128), F32),
                pltpu.VMEM((2, 2, 48, 4, 128), BF16),
                pltpu.VMEM((2, 4, 48, 4, 128), BF16),
                pltpu.VMEM((2, 48, 16, 128), F32),
                pltpu.VMEM((16, 38, 16, 128), BF16),
                pltpu.VMEM((16, 2, 18, 16, 128), BF16),
                pltpu.VMEM((4, 2, 288, 128), F32),
                pltpu.VMEM((4, 288, 256), BF16),
                pltpu.VMEM((4, 2, 192, 128), F32),
                pltpu.VMEM((4, 192, 256), BF16),
                pltpu.VMEM((2, 288, 256), F32),
                pltpu.VMEM((16, 4, 8, 8, 128), F32),
                pltpu.VMEM((16, 8, 8, 128), F32),
                pltpu.VMEM((16, 8, 128), F32),
                pltpu.VMEM((2, 16, 128), F32),
                pltpu.VMEM((2, 16, 128), BF16),
                pltpu.VMEM((2, ns, 16, 128), BF16),
                pltpu.VMEM((16, 128), F32),
                pltpu.VMEM((16, 128), F32),
                pltpu.VMEM((16, 32, 128), F32),
                pltpu.VMEM((ns + 1, 16, 128), BF16),
                pltpu.VMEM((ns, 2, 16, 128), BF16),
                pltpu.VMEM((ns, 16, 128), BF16),
                pltpu.VMEM((2, 3, 40, 16), F32),
                pltpu.VMEM((2, 2, 48, 128), F32),
                pltpu.VMEM((2, 16, 128), F32),
                pltpu.VMEM((256, 256), BF16),
                pltpu.VMEM((8, 256), F32),
                pltpu.VMEM((8, 256), BF16),
                pltpu.VMEM((ns, 8, 256), BF16),
                pltpu.VMEM((192, 8 * ns), BF16),
                dma, dma((5,)), dma((14,)), dma((14,)), dma((2,)), dma((2,)), dma, dma, dma, dma, dma, dma,
            ],
            compiler_params=pltpu.CompilerParams(
                collective_id=0, has_side_effects=True, vmem_limit_bytes=40 * 2**20),
        )(*[pltpu.with_memory_space_constraint(x, pltpu.HBM) for x in (
            by_tap(first_kernel), by_tap(second_kernel), density_weight, upsample_kernel, color_weight.T, volume)])
        return out

    placed = (P(None, "slab", "tile", None), P(), P(), P(), P(), P())
    return jax.shard_map(
        body, mesh=mesh, in_specs=placed, out_specs=P(None, "tile", None), check_vma=False
    )
```
